128 devices in a mesh: band: 16 (over z, y), slab: 8 (over x, core).
Axes of the slice: x: 4, y: 4, z: 4, core: 2. Of those that a mesh axis runs over, the one named last changes fastest.
Arguments:
- orbitals: float32 [64, 96, 18432], P('band', 'slab'), may hold values from -0.07 to 0.07
- potential: float32 [96, 9216], P('slab'), may hold values from -6 to 2
Outputs:
- evolved: float32 [64, 96, 18432], P('band', 'slab')
- hartree: float32 [96, 9216], P('slab')
The draws below stay inside these ranges and needn't reach their ends.
All inputs are finite; a program needn't handle non-finite values.
Results may differ from the reference program's by a relative error of at most 0.0003.
Values sent between devices are 32-bit elements; how exact they have to be, the bound alone decides.
A program may use at most 128 MiB of HBM per device.

```python
import math
import jax
import jax.numpy as jnp
from jax import lax

GRID = 96
BANDS = 64


def block_scale(key, extent, split, smallest, high):
    def one(dim, shards_of):
        draws = jax.random.uniform(jax.random.fold_in(jax.random.fold_in(key, 6), dim), (shards_of,), jnp.float32, smallest / len(split), high / len(split))
        return jnp.repeat(jnp.exp(draws), extent[dim] // shards_of).reshape((-1,) + (1,) * (len(extent) - dim - 1))

    factor_of = one(*split[0])
    for cut in split[1:]:
        factor_of = factor_of * one(*cut)
    return factor_of


def gaussian(own_key, extent, deviation, reach, shards=(), held_as=jnp.bfloat16):
    level = block_scale(own_key, extent, shards, -0.22, 0.18) if shards else 1.0
    result = jax.random.normal(own_key, extent, jnp.float32) * deviation * level
    return jnp.minimum(jnp.maximum(result, -reach), reach).astype(held_as)


def setup_inputs(seed: int = 0) -> dict:
    key_list = jax.random.split(jax.random.key(seed), 3)
    orbitals = gaussian(key_list[0], (BANDS, GRID, 2 * GRID * GRID), 0.012, 0.07, ((0, 16), (1, 8)), jnp.float32)
    potential = jnp.clip(-6.0 + 8.0 * jax.random.uniform(key_list[1], (GRID, GRID * GRID), jnp.float32) ** block_scale(key_list[1], (GRID, GRID * GRID), ((0, 8),), -0.2, 0.2), -6.0, 2.0)
    return {"orbitals": orbitals, "potential": potential}


TIME_STEP = 0.1


def wave(length):
    index = jnp.arange(length, dtype=jnp.int32)
    signed = (index + length // 2) % length - length // 2
    return signed, signed.astype(jnp.float32) * (2.0 * math.pi / length)


def reference(orbitals, potential):
    signed, wave_k = wave(GRID)
    square = wave_k * wave_k
    ksq = square[:, None, None] + square[None, :, None] + square[None, None, :]
    phase_angle = ksq * (TIME_STEP / 4)
    rotor = lax.complex(jnp.cos(phase_angle), -jnp.sin(phase_angle))

    def half_step(pair):
        psi = lax.complex(pair[..., :GRID], pair[..., GRID:])
        out = jnp.fft.ifftn(jnp.fft.fftn(psi) * rotor)
        return jnp.concatenate([jnp.real(out), jnp.imag(out)], -1)

    grids = orbitals.reshape(BANDS, GRID, GRID, 2 * GRID)
    moved = lax.map(half_step, grids)
    real_part = moved[..., :GRID]
    imag_part = moved[..., GRID:]
    density = jnp.sum(real_part * real_part + imag_part * imag_part, axis=0)
    anchor = (signed[:, None, None] == 0) & (signed[None, :, None] == 0) & (signed[None, None, :] == 0)
    factor = jnp.where(anchor, 0.0, 4.0 * math.pi / jnp.where(anchor, 1.0, ksq)).astype(jnp.float32)
    hartree = jnp.real(jnp.fft.ifftn(jnp.fft.fftn(density) * factor))
    angle = (potential.reshape(GRID, GRID, GRID) + hartree) * TIME_STEP
    cosine = jnp.cos(angle)
    sine = jnp.sin(angle)
    kicked = jnp.concatenate([real_part * cosine + imag_part * sine, imag_part * cosine - real_part * sine], -1)
    evolved = lax.map(half_step, kicked)
    return evolved.reshape(BANDS, GRID, 2 * GRID * GRID), hartree.reshape(GRID, GRID * GRID)
```

```python
import functools
import math

import jax
import jax.numpy as jnp
import ml_dtypes
import numpy as np
from jax import lax
from jax.experimental import pallas as pl
from jax.experimental.pallas import tpu as pltpu
from jax.sharding import PartitionSpec as P

GRID = 96
TIME_STEP = 0.1
MESH = pl.DeviceIdType.MESH
SLABS = 8
GROUPS = 16
BANDS = 4
OWN = GRID // SLABS
LINE = OWN * GRID
TILES = LINE // 128
BLOCK = TILES * 2 * OWN
BAND = SLABS * BLOCK
PAIRS = GRID // 2
SHARE = GRID // GROUPS
F32 = jnp.float32
BF16 = jnp.bfloat16


def half_step_factor():
    n = np.arange(GRID)
    m = (n + GRID // 2) % GRID - GRID // 2
    k = 2.0 * math.pi / GRID * m
    phase = np.exp(-1j * k * k * TIME_STEP / 4)
    diff = (n[:, None] - n[None, :]) % GRID
    line = np.fft.ifft(phase)
    full = line[diff]
    out = np.zeros((2, GRID, 2, GRID))
    out[0, :, 0] = full.real
    out[0, :, 1] = -full.imag
    out[1, :, 0] = full.imag
    out[1, :, 1] = full.real
    return out


def real_basis():
    n = np.arange(GRID)
    rows, ksq = [np.full(GRID, 1.0 / math.sqrt(GRID))], [0.0]
    for m in range(1, GRID // 2):
        angle = 2.0 * math.pi * ((m * n) % GRID) / GRID
        rows += [np.cos(angle) * math.sqrt(2.0 / GRID), np.sin(angle) * math.sqrt(2.0 / GRID)]
        ksq += [(2.0 * math.pi * m / GRID) ** 2] * 2
    rows.append(np.where(n % 2 == 0, 1.0, -1.0) / math.sqrt(GRID))
    ksq.append(math.pi**2)
    return np.stack(rows), np.array(ksq)


def split(matrix):
    high = matrix.astype(np.float32).astype(ml_dtypes.bfloat16)
    low = (matrix - high.astype(np.float64)).astype(ml_dtypes.bfloat16)
    return np.stack([high, low])


@functools.lru_cache(maxsize=None)
def tables():
    g = half_step_factor()
    t = {}
    into = g.transpose(2, 3, 0, 1)
    padded = np.zeros((2, GRID, 2, 128))
    padded[..., :GRID] = into
    padded = padded.reshape(2 * GRID, 256)
    za = np.zeros((2, 256, 256))
    za[0, :192] = padded
    za[1, 64:] = padded
    t["z_in"] = np.stack([split(za[0]), split(za[1])]).reshape(4 * 256, 256)
    rows = np.zeros((2, 128, 2, GRID))
    rows[:, :GRID] = into
    rows = rows.reshape(256, 2 * GRID)
    zb = np.zeros((2, 256, 256))
    zb[0, :, :192] = rows
    zb[1, :, 64:] = rows
    t["z_out"] = np.stack([split(zb[0]), split(zb[1])]).reshape(4 * 256, 256)
    j, s, a = np.meshgrid(np.arange(4), np.arange(SLABS), np.arange(3), indexing="ij")
    wire_y = 12 * s + 4 * a + j
    pair_y = 2 * np.arange(PAIRS)[None, :] + np.arange(2)[:, None]
    ky = g[:, wire_y][:, :, :, :, :, pair_y]
    t["y_in"] = split(ky.transpose(1, 0, 2, 3, 5, 4, 6).reshape(192, 192)).reshape(384, 192)
    ky = g[:, pair_y][:, :, :, :, wire_y]
    t["y_out"] = split(ky.transpose(1, 0, 2, 4, 3, 5, 6).reshape(192, 192)).reshape(384, 192)
    kx = g.reshape(2, GRID, 2, SLABS, OWN)
    t["x_in"] = split(kx.transpose(0, 1, 3, 2, 4).reshape(192, 192)).reshape(384, 192)
    kx = g.reshape(2, SLABS, OWN, 2, GRID)
    t["x_out"] = split(kx.transpose(1, 0, 2, 3, 4).reshape(192, 192)).reshape(384, 192)
    q, ksq = real_basis()
    qx = np.zeros((GROUPS, 8, GRID))
    qx[:, :SHARE] = q.reshape(GROUPS, SHARE, GRID)
    qx = qx.reshape(128, GRID)
    t["qx"] = split(qx).reshape(256, GRID)
    t["qxt"] = split(qx.T).reshape(192, 128)
    qz = np.zeros((128, 128))
    qz[:GRID, :GRID] = q.T
    t["qz"] = split(qz).reshape(256, 128)
    t["qzt"] = split(qz.T).reshape(256, 128)
    aj_s = 12 * np.arange(SLABS)[None, :] + np.arange(OWN)[:, None]
    t["qy"] = split(q[:, aj_s.reshape(-1)]).reshape(192, GRID)
    qyt = np.zeros((SLABS, 16, GRID))
    qyt[:, :OWN] = q.T.reshape(SLABS, OWN, GRID)
    t["qyt"] = split(qyt).transpose(1, 0, 2, 3).reshape(SLABS, 32, GRID)
    kxz = np.ones((GROUPS, 8, 128))
    kxz[:, :SHARE, :GRID] = ksq.reshape(GROUPS, SHARE)[:, :, None] + ksq[None, None, :]
    t["kxz"] = kxz.astype(np.float32)
    t["ky2"] = np.broadcast_to(ksq[:, None], (GRID, 128)).astype(np.float32)
    return t


NAMES = ("z_in", "z_out", "y_in", "y_out", "x_in", "x_out", "qx", "qxt", "qz", "qzt", "qy", "qyt", "kxz", "ky2")


def halves(x):
    high = x.astype(BF16)
    return high, (x - high.astype(F32)).astype(BF16)


def dot(a, b):
    return jnp.dot(a, b, preferred_element_type=F32)


def times(x, high, low):
    xh, xl = halves(x)
    return dot(xh, high) + (dot(xl, high) + dot(xh, low))


def left(high, low, x):
    xh, xl = halves(x)
    return dot(high, xh) + (dot(high, xl) + dot(low, xh))


def sin_cos(t):
    n = jnp.round(t * (2.0 / math.pi))
    r = t - n * 1.5703125
    r = r - n * 4.8375129699707031e-4
    r = r - n * 7.5495649e-08
    r2 = r * r
    sine = r + r * r2 * (-1.6666654611e-1 + r2 * (8.3321608736e-3 + r2 * -1.9515295891e-4))
    cosine = 1.0 - 0.5 * r2 + r2 * r2 * (4.166664568298827e-2 + r2 * (-1.388731625493765e-3 + r2 * 2.443315711809948e-5))
    quarter = n.astype(jnp.int32) & 3
    odd = (quarter & 1) == 1
    s = jnp.where(odd, cosine, sine)
    c = jnp.where(odd, sine, cosine)
    s = jnp.where(quarter >= 2, -s, s)
    c = jnp.where((quarter == 1) | (quarter == 2), -c, c)
    return s, c


def lane_of(shape):
    return lax.broadcasted_iota(jnp.int32, shape, len(shape) - 1)


def packed(parts):
    lane = lane_of(parts[0].shape)
    r1 = pltpu.roll(parts[1], 96, 1)
    r2 = pltpu.roll(parts[2], 64, 1)
    r3 = pltpu.roll(parts[3], 32, 1)
    return (
        jnp.where(lane < 96, parts[0], r1),
        jnp.where(lane < 64, r1, r2),
        jnp.where(lane < 32, r2, r3),
    )


def unpacked(tiles):
    lane = lane_of(tiles[0].shape)
    return (
        tiles[0],
        pltpu.roll(jnp.where(lane < 64, tiles[1], tiles[0]), 32, 1),
        pltpu.roll(jnp.where(lane < 32, tiles[2], tiles[1]), 64, 1),
        pltpu.roll(tiles[2], 96, 1),
    )


def kernel(orb, pot, z_in, z_out, y_in, y_out, x_in, x_out, qx, qxt, qz, qzt, qy, qyt, kxz, ky2,
           ev, har,
           ib, plane, wire, lines, moved, back, home, ob, dens, dq, part, share, modes, whole, zt, green, hq, hart,
           vb, vl, cosb, sinb, hs,
           in_sem, out_sem, pot_s, pot_r, w_s, w_r, b_s, b_r, rs_s, rs_r, ag_s, ag_r, hq_s, hq_r, h_s, h_r, own_sem):
    me = lax.axis_index("slab")
    grp = lax.axis_index("band")
    slab_peers = [(d, lax.rem(me + d, SLABS)) for d in range(1, SLABS)]
    band_peers = [(d, lax.rem(grp + d, GROUPS)) for d in range(1, GROUPS)]

    barrier = pltpu.get_barrier_semaphore()
    for _, q in slab_peers:
        pl.semaphore_signal(barrier, inc=1, device_id={"slab": q}, device_id_type=MESH)
    for _, q in band_peers:
        pl.semaphore_signal(barrier, inc=1, device_id={"band": q}, device_id_type=MESH)

    def load(b):
        return pltpu.make_async_copy(orb.at[b], ib.at[b], in_sem.at[b])

    for b in range(BANDS):
        load(b).start()

    def slab_copy(src, dst, s, r, q):
        return pltpu.make_async_remote_copy(src, dst, s, r, device_id={"slab": q}, device_id_type=MESH)

    def band_copy(src, dst, s, r, q):
        return pltpu.make_async_remote_copy(src, dst, s, r, device_id={"band": q}, device_id_type=MESH)

    def first(b, carry):
        load(b).wait()

        rest = jnp.zeros((16 - OWN, 256), F32)

        def kz(chunk, carry):
            start = pl.multiple_of(chunk * (8 * 384), 128)
            for j in range(2):
                x = jnp.concatenate(
                    [piece for i in range(8) for piece in (ib[b, :, pl.ds(start + 384 * i + 128 * j, 256)], rest)], 0
                )
                r = times(x, z_in[pl.ds(512 * j, 256)], z_in[pl.ds(512 * j + 256, 256)])
                for c in range(2):
                    row = pl.multiple_of(768 * (2 * j + c) + chunk * 128, 128)
                    plane[pl.ds(row, 128)] = r[:, 128 * c : 128 * c + 128]
            return carry

        lax.fori_loop(0, 6, kz, 0)

        def ky(pair, carry):
            cols = []
            for i in range(2):
                x = 2 * pair + i
                cols.append(
                    jnp.concatenate([plane[pl.ds(768 * k + x, PAIRS, stride=16), :] for k in range(4)], 0)
                )
            r = left(y_in[pl.ds(0, 192)], y_in[pl.ds(192, 192)], jnp.concatenate(cols, 1))
            for i in range(2):
                x = 2 * pair + i
                tiles = packed([r[48 * j : 48 * j + 48, 128 * i : 128 * i + 128] for j in range(4)])
                for t in range(3):
                    for c in range(2):
                        wire[pl.ds(b * BAND + t * 24 + c * OWN + x, 24, stride=72), :] = tiles[t][24 * c : 24 * c + 24]
            return carry

        lax.fori_loop(0, OWN // 2, ky, 0)

        @pl.when(b == 0)
        def _():
            pl.semaphore_wait(barrier, SLABS - 1 + GROUPS - 1)

        for d, q in slab_peers:
            send_line(b, d, q).start()
        own_line(b).start()
        return carry

    def send_line(b, d, q):
        return slab_copy(
            wire.at[pl.ds(b * BAND + q * BLOCK, BLOCK)],
            lines.at[pl.ds(b * BAND + me * BLOCK, BLOCK)],
            w_s.at[b, d],
            w_r.at[b, d],
            q,
        )

    def own_line(b):
        at = pl.ds(b * BAND + me * BLOCK, BLOCK)
        return pltpu.make_async_copy(wire.at[at], lines.at[at], own_sem.at[b])

    lax.fori_loop(0, BANDS, first, 0)

    def send_pot(d, q):
        return slab_copy(
            pot.at[:, pl.ds(pl.multiple_of(q * LINE, 128), LINE)], vb.at[me], pot_s.at[d], pot_r.at[d], q
        )

    for d, q in slab_peers:
        send_pot(d, q).start()
    own_pot = pltpu.make_async_copy(
        pot.at[:, pl.ds(pl.multiple_of(me * LINE, 128), LINE)], vb.at[me], own_sem.at[BANDS]
    )
    own_pot.start()

    for i in range(8):
        ksq = ky2[...] + kxz[grp, i : i + 1, :]
        zero = ksq == 0.0
        green[:, 128 * i : 128 * i + 128] = jnp.where(zero, 0.0, 4.0 * math.pi / jnp.where(zero, 1.0, ksq))

    dens[...] = jnp.zeros_like(dens)

    def lines_x(b, carry):
        own_line(b).wait()
        for d, q in slab_peers:
            send_line(b, d, q).wait_recv()

        def kx(a, carry):
            x = jnp.concatenate(
                [
                    jnp.concatenate(
                        [lines[pl.ds(b * BAND + s * BLOCK + (3 * a + t) * 24, 24)] for s in range(SLABS)], 0
                    )
                    for t in range(3)
                ],
                1,
            )
            r = left(x_in[pl.ds(0, 192)], x_in[pl.ds(192, 192)], x)
            at = pl.ds(pl.multiple_of(a * 384, 128), 384)
            moved[b, :, at] = r
            dens[:, at] += r[:GRID] * r[:GRID] + r[GRID:] * r[GRID:]
            return carry

        lax.fori_loop(0, 3, kx, 0)
        return carry

    lax.fori_loop(0, BANDS, lines_x, 0)

    dq[...] = left(qx[pl.ds(0, 128)], qx[pl.ds(128, 128)], dens[...])

    def send_part(d, q):
        return band_copy(dq.at[pl.ds(pl.multiple_of(q * 8, 8), 8)], part.at[grp], rs_s.at[d], rs_r.at[d], q)

    for d, q in band_peers:
        send_part(d, q).start()
    total = dq[pl.ds(pl.multiple_of(grp * 8, 8), 8)]
    own_pot.wait()
    for d, q in slab_peers:
        send_pot(d, q).wait_recv()
    for s in range(SLABS):
        vl[OWN * s : OWN * s + OWN, :] = vb[s]
    for d, q in band_peers:
        send_part(d, q).wait_recv()
    for d, q in band_peers:
        total = total + part[q]
    share[...] = total

    def send_share(d, q):
        return slab_copy(share, whole.at[me], ag_s.at[d], ag_r.at[d], q)

    for d, q in slab_peers:
        send_share(d, q).start()
    whole[me] = total
    for d, q in slab_peers:
        send_share(d, q).wait_recv()
    for a in range(3):
        tiles = [
            jnp.concatenate([whole[s, :, 384 * a + 128 * t : 384 * a + 128 * t + 128] for s in range(SLABS)], 0)
            for t in range(3)
        ]
        x = jnp.concatenate(unpacked(tiles), 0)
        zt[pl.ds(256 * a, 256)] = times(x, qz[pl.ds(0, 128)], qz[pl.ds(128, 128)])
    x = jnp.concatenate([zt[pl.ds(i, GRID, stride=8), :] for i in range(8)], 1)
    x = left(qy[pl.ds(0, GRID)], qy[pl.ds(GRID, GRID)], x) * green[...]
    x = left(qyt[me, 0:16], qyt[me, 16:32], x)
    x = jnp.concatenate([x[:, 128 * i : 128 * i + 128] for i in range(8)], 0)
    zt[pl.ds(0, 128)] = times(x, qzt[pl.ds(0, 128)], qzt[pl.ds(128, 128)])
    for a in range(3):
        tiles = packed([zt[pl.ds(4 * a + j, 8, stride=16), :] for j in range(4)])
        for t in range(3):
            modes[:, 384 * a + 128 * t : 384 * a + 128 * t + 128] = tiles[t]

    def send_modes(d, q):
        return band_copy(modes, hq.at[pl.ds(pl.multiple_of(grp * 8, 8), 8)], hq_s.at[d], hq_r.at[d], q)

    for d, q in band_peers:
        send_modes(d, q).start()
    hq[pl.ds(pl.multiple_of(grp * 8, 8), 8)] = modes[...]
    for d, q in band_peers:
        send_modes(d, q).wait_recv()
    h = left(qxt[pl.ds(0, GRID)], qxt[pl.ds(GRID, GRID)], hq[...])
    hart[...] = h
    s, c = sin_cos((vl[...] + h) * TIME_STEP)
    sinb[...] = s
    cosb[...] = c

    def send_back(b, d, q):
        return slab_copy(
            back.at[pl.ds(b * BAND + q * BLOCK, BLOCK)],
            home.at[pl.ds(b * BAND + me * BLOCK, BLOCK)],
            b_s.at[b, d],
            b_r.at[b, d],
            q,
        )

    def own_back(b):
        at = pl.ds(b * BAND + me * BLOCK, BLOCK)
        return pltpu.make_async_copy(back.at[at], home.at[at], own_sem.at[b])

    def kick(b, carry):
        def kx(a, carry):
            at = pl.ds(pl.multiple_of(a * 384, 128), 384)
            re = moved[b, 0:GRID, at]
            im = moved[b, GRID : 2 * GRID, at]
            cs = cosb[:, at]
            sn = sinb[:, at]
            x = jnp.concatenate([re * cs + im * sn, im * cs - re * sn], 0)
            r = left(x_out[pl.ds(0, 192)], x_out[pl.ds(192, 192)], x)
            for q in range(SLABS):
                for t in range(3):
                    back[pl.ds(b * BAND + q * BLOCK + (3 * a + t) * 24, 24)] = r[24 * q : 24 * q + 24, 128 * t : 128 * t + 128]
            return carry

        lax.fori_loop(0, 3, kx, 0)
        for d, q in slab_peers:
            send_back(b, d, q).start()
        own_back(b).start()
        return carry

    lax.fori_loop(0, BANDS, kick, 0)

    for q in range(SLABS):
        hs[q] = hart[OWN * q : OWN * q + OWN, :]

    def send_hart(d, q):
        return slab_copy(
            hs.at[q], har.at[:, pl.ds(pl.multiple_of(me * LINE, 128), LINE)], h_s.at[d], h_r.at[d], q
        )

    for d, q in slab_peers:
        send_hart(d, q).start()
    own_hart = pltpu.make_async_copy(
        hs.at[me], har.at[:, pl.ds(pl.multiple_of(me * LINE, 128), LINE)], own_sem.at[BANDS]
    )
    own_hart.start()

    def store(b):
        return pltpu.make_async_copy(ob.at[b], ev.at[b], out_sem.at[b])

    def last(b, carry):
        own_back(b).wait()
        for d, q in slab_peers:
            send_back(b, d, q).wait_recv()

        def ky(pair, carry):
            cols = []
            for i in range(2):
                x = 2 * pair + i
                tiles = [
                    jnp.concatenate(
                        [home[pl.ds(b * BAND + t * 24 + c * OWN + x, 24, stride=72), :] for c in range(2)], 0
                    )
                    for t in range(3)
                ]
                cols.append(jnp.concatenate(unpacked(tiles), 0))
            r = left(y_out[pl.ds(0, 192)], y_out[pl.ds(192, 192)], jnp.concatenate(cols, 1))
            for i in range(2):
                x = 2 * pair + i
                for k in range(4):
                    plane[pl.ds(768 * k + x, PAIRS, stride=16), :] = r[48 * k : 48 * k + 48, 128 * i : 128 * i + 128]
            return carry

        lax.fori_loop(0, OWN // 2, ky, 0)

        def kz(chunk, carry):
            res = []
            for j in range(2):
                x = jnp.concatenate(
                    [plane[pl.ds(pl.multiple_of(768 * (2 * j + c) + chunk * 128, 128), 128)] for c in range(2)], 1
                )
                res.append(times(x, z_out[pl.ds(512 * j, 256)], z_out[pl.ds(512 * j + 256, 256)]))
            tiles = (res[0][:, :128], res[0][:, 128:] + res[1][:, :128], res[1][:, 128:])
            start = pl.multiple_of(chunk * (8 * 384), 128)
            for i in range(8):
                for t in range(3):
                    ob[b, :, pl.ds(start + 384 * i + 128 * t, 128)] = tiles[t][16 * i : 16 * i + OWN]
            return carry

        lax.fori_loop(0, 6, kz, 0)
        store(b).start()
        return carry

    lax.fori_loop(0, BANDS, last, 0)

    own_hart.wait()
    for d, q in slab_peers:
        send_hart(d, q).wait()
        send_pot(d, q).wait_send()
        send_share(d, q).wait_send()
    for d, q in band_peers:
        send_part(d, q).wait_send()
        send_modes(d, q).wait_send()

    def drain(b, carry):
        for d, q in slab_peers:
            send_line(b, d, q).wait_send()
            send_back(b, d, q).wait_send()
        store(b).wait()
        return carry

    lax.fori_loop(0, BANDS, drain, 0)


def body(orbitals, potential):
    t = tables()
    consts = [jnp.asarray(t[name]) for name in NAMES]
    vmem = lambda *shape: pltpu.VMEM(shape, F32)
    dma = lambda *shape: pltpu.SemaphoreType.DMA(shape)
    ev, har = pl.pallas_call(
        kernel,
        out_shape=(
            jax.ShapeDtypeStruct(orbitals.shape, F32),
            jax.ShapeDtypeStruct(potential.shape, F32),
        ),
        in_specs=[pl.BlockSpec(memory_space=pl.ANY)] * 2 + [pl.BlockSpec(memory_space=pltpu.VMEM)] * len(consts),
        out_specs=[pl.BlockSpec(memory_space=pl.ANY)] * 2,
        scratch_shapes=[
            vmem(BANDS, OWN, 2 * GRID * GRID),
            vmem(4 * 768, 128),
            vmem(BANDS * BAND, 128),
            vmem(BANDS * BAND, 128),
            vmem(BANDS, 2 * GRID, LINE),
            vmem(BANDS * BAND, 128),
            vmem(BANDS * BAND, 128),
            vmem(BANDS, OWN, 2 * GRID * GRID),
            vmem(GRID, LINE),
            vmem(128, LINE),
            vmem(GROUPS, 8, LINE),
            vmem(8, LINE),
            vmem(8, LINE),
            vmem(SLABS, 8, LINE),
            vmem(768, 128),
            vmem(GRID, 1024),
            vmem(128, LINE),
            vmem(GRID, LINE),
            vmem(SLABS, OWN, LINE),
            vmem(GRID, LINE),
            vmem(GRID, LINE),
            vmem(GRID, LINE),
            vmem(SLABS, OWN, LINE),
            dma(BANDS), dma(BANDS),
            dma(SLABS), dma(SLABS),
            dma(BANDS, SLABS), dma(BANDS, SLABS),
            dma(BANDS, SLABS), dma(BANDS, SLABS),
            dma(GROUPS), dma(GROUPS),
            dma(SLABS), dma(SLABS),
            dma(GROUPS), dma(GROUPS),
            dma(SLABS), dma(SLABS),
            dma(BANDS + 1),
        ],
        compiler_params=pltpu.CompilerParams(
            collective_id=0, has_side_effects=True, vmem_limit_bytes=56 * 1024 * 1024
        ),
    )(orbitals, potential, *consts)
    return ev, har


def solution(mesh):
    return jax.shard_map(
        body,
        mesh=mesh,
        in_specs=(P("band", "slab", None), P("slab", None)),
        out_specs=(P("band", "slab", None), P("slab", None)),
        check_vma=False,
    )
```

```python
import functools
import math

import jax
import jax.numpy as jnp
import ml_dtypes
import numpy as np
from jax import lax
from jax.experimental import pallas as pl
from jax.experimental.pallas import tpu as pltpu
from jax.sharding import PartitionSpec as P

GRID = 96
TIME_STEP = 0.1
MESH = pl.DeviceIdType.MESH
SLABS = 8
GROUPS = 16
BANDS = 4
OWN = GRID // SLABS
LINE = OWN * GRID
TILES = LINE // 128
BLOCK = TILES * 2 * OWN
BAND = SLABS * BLOCK
XROWS = 2 * GRID * GRID // 128 * BANDS
PAIRS = GRID // 2
SHARE = GRID // GROUPS
SCALE = 1.88474
F32 = jnp.float32
BF16 = jnp.bfloat16


def half_step_line():
    n = np.arange(GRID)
    m = (n + GRID // 2) % GRID - GRID // 2
    k = 2.0 * math.pi / GRID * m
    phase = np.exp(-1j * k * k * TIME_STEP / 4)
    exact = np.fft.ifft(phase) / SCALE
    line = np.stack([exact.real, exact.imag]).astype(np.float32).astype(ml_dtypes.bfloat16).astype(np.float64)

    def worst(values):
        return np.abs(np.fft.fft((values[0] + 1j * values[1]) * SCALE) - phase).max()

    now = worst(line)
    for _ in range(3):
        for part in range(2):
            for t in range(GRID // 2 + 1):
                for sign in (1.0, -1.0):
                    trial = line.copy()
                    step = 2.0 ** (math.floor(math.log2(abs(line[part, t]))) - 7)
                    trial[part, [t, -t % GRID]] = line[part, t] + sign * step
                    error = worst(trial)
                    if error < 0.9999 * now:
                        now, line = error, trial
    return line


def half_step_factor():
    n = np.arange(GRID)
    real, imag = half_step_line()[:, (n[:, None] - n[None, :]) % GRID]
    out = np.zeros((2, GRID, 2, GRID))
    out[0, :, 0] = real
    out[0, :, 1] = -imag
    out[1, :, 0] = imag
    out[1, :, 1] = real
    return out


def real_basis():
    n = np.arange(GRID)
    rows, ksq = [np.full(GRID, 1.0 / math.sqrt(GRID))], [0.0]
    for m in range(1, GRID // 2):
        angle = 2.0 * math.pi * ((m * n) % GRID) / GRID
        rows += [np.cos(angle) * math.sqrt(2.0 / GRID), np.sin(angle) * math.sqrt(2.0 / GRID)]
        ksq += [(2.0 * math.pi * m / GRID) ** 2] * 2
    rows.append(np.where(n % 2 == 0, 1.0, -1.0) / math.sqrt(GRID))
    ksq.append(math.pi**2)
    return np.stack(rows), np.array(ksq)


def exact(matrix):
    return matrix.astype(ml_dtypes.bfloat16)


def split(matrix):
    high = matrix.astype(np.float32).astype(ml_dtypes.bfloat16)
    low = (matrix - high.astype(np.float64)).astype(ml_dtypes.bfloat16)
    return np.stack([high, low])


@functools.lru_cache(maxsize=None)
def tables():
    g = half_step_factor()
    t = {}
    into = g.transpose(2, 3, 0, 1)
    padded = np.zeros((2, GRID, 2, 128))
    padded[..., :GRID] = into
    padded = padded.reshape(2 * GRID, 256)
    za = np.zeros((2, 256, 256))
    za[0, :192] = padded
    za[1, 64:] = padded
    t["z_in"] = exact(za.reshape(512, 256))
    rows = np.zeros((2, 128, 2, GRID))
    rows[:, :GRID] = into
    rows = rows.reshape(256, 2 * GRID)
    zb = np.zeros((2, 256, 256))
    zb[0, :, :192] = rows
    zb[1, :, 64:] = rows
    t["z_out"] = exact(zb.reshape(512, 256))
    j, s, a = np.meshgrid(np.arange(4), np.arange(SLABS), np.arange(3), indexing="ij")
    wire_y = 12 * s + 4 * a + j
    pair_y = 2 * np.arange(PAIRS)[None, :] + np.arange(2)[:, None]
    ky = g[:, wire_y][:, :, :, :, :, pair_y]
    t["y_in"] = exact(ky.transpose(1, 0, 2, 3, 5, 4, 6).reshape(192, 192))
    ky = g[:, pair_y][:, :, :, :, wire_y]
    t["y_out"] = exact(ky.transpose(1, 0, 2, 4, 3, 5, 6).reshape(192, 192))
    kx = g.reshape(2, GRID, 2, SLABS, OWN)
    t["x_in"] = exact(kx.transpose(0, 1, 3, 2, 4).reshape(192, 192))
    kx = g.reshape(2, SLABS, OWN, 2, GRID)
    t["x_out"] = exact(kx.transpose(1, 0, 2, 3, 4).reshape(192, 192))
    q, ksq = real_basis()
    qx = np.zeros((GROUPS, 8, GRID))
    qx[:, :SHARE] = q.reshape(GROUPS, SHARE, GRID)
    qx = qx.reshape(128, GRID)
    t["qx"] = split(qx * SCALE**6).reshape(256, GRID)
    t["qxt"] = split(qx.T).reshape(192, 128)
    qz = np.zeros((128, 128))
    qz[:GRID, :GRID] = q.T
    t["qz"] = split(qz).reshape(256, 128)
    t["qzt"] = split(qz.T).reshape(256, 128)
    aj_s = 12 * np.arange(SLABS)[None, :] + np.arange(OWN)[:, None]
    t["qy"] = split(q[:, aj_s.reshape(-1)]).reshape(192, GRID)
    qyt = np.zeros((SLABS, 16, GRID))
    qyt[:, :OWN] = q.T.reshape(SLABS, OWN, GRID)
    t["qyt"] = split(qyt).transpose(1, 0, 2, 3).reshape(SLABS, 32, GRID)
    kxz = np.ones((GROUPS, 8, 128))
    kxz[:, :SHARE, :GRID] = ksq.reshape(GROUPS, SHARE)[:, :, None] + ksq[None, None, :]
    t["kxz"] = kxz.astype(np.float32)
    t["ky2"] = np.broadcast_to(ksq[:, None], (GRID, 128)).astype(np.float32)
    return t


NAMES = ("z_in", "y_in", "x_in", "kxz", "ky2", "qx", "qz", "qy", "qyt", "qzt", "qxt", "x_out", "y_out", "z_out")


def halves(x):
    high = x.astype(BF16)
    return high, (x - high.astype(F32)).astype(BF16)


def dot(a, b):
    return jnp.dot(a, b, preferred_element_type=F32)


def times(x, high, low):
    xh, xl = halves(x)
    return dot(xh, high) + (dot(xl, high) + dot(xh, low))


def left(high, low, x):
    xh, xl = halves(x)
    return dot(high, xh) + (dot(high, xl) + dot(low, xh))


def sin_cos(t):
    n = jnp.round(t * (2.0 / math.pi))
    r = t - n * 1.5703125
    r = r - n * 4.8375129699707031e-4
    r = r - n * 7.5495649e-08
    r2 = r * r
    sine = r + r * r2 * (-1.6666654611e-1 + r2 * (8.3321608736e-3 + r2 * -1.9515295891e-4))
    cosine = 1.0 - 0.5 * r2 + r2 * r2 * (4.166664568298827e-2 + r2 * (-1.388731625493765e-3 + r2 * 2.443315711809948e-5))
    quarter = n.astype(jnp.int32) & 3
    odd = (quarter & 1) == 1
    s = jnp.where(odd, cosine, sine)
    c = jnp.where(odd, sine, cosine)
    s = jnp.where(quarter >= 2, -s, s)
    c = jnp.where((quarter == 1) | (quarter == 2), -c, c)
    return s, c


def times2(x, table):
    r = dot(jnp.concatenate(halves(x), 0), table)
    return r[: x.shape[0]] + r[x.shape[0] :]


def left2(table, x):
    r = dot(table, jnp.concatenate(halves(x), 1))
    return r[:, : x.shape[1]] + r[:, x.shape[1] :]


def lane_of(shape):
    return lax.broadcasted_iota(jnp.int32, shape, len(shape) - 1)


def packed(parts):
    lane = lane_of(parts[0].shape)
    r1 = pltpu.roll(parts[1], 96, 1)
    r2 = pltpu.roll(parts[2], 64, 1)
    r3 = pltpu.roll(parts[3], 32, 1)
    return (
        jnp.where(lane < 96, parts[0], r1),
        jnp.where(lane < 64, r1, r2),
        jnp.where(lane < 32, r2, r3),
    )


def unpacked(tiles):
    lane = lane_of(tiles[0].shape)
    return (
        tiles[0],
        pltpu.roll(jnp.where(lane < 64, tiles[1], tiles[0]), 32, 1),
        pltpu.roll(jnp.where(lane < 32, tiles[2], tiles[1]), 64, 1),
        pltpu.roll(tiles[2], 96, 1),
    )


def kernel(orb, pot, *refs):
    sources, refs = refs[: len(NAMES)], refs[len(NAMES) :]
    ev, har, refs = refs[0], refs[1], refs[2:]
    consts, refs = refs[: len(NAMES)], refs[len(NAMES) :]
    z_in, y_in, x_in, kxz, ky2, qx, qz, qy, qyt, qzt, qxt, x_out, y_out, z_out = consts
    (
     ib, wire, lines, moved, back, home, ob, dens, dq, part, share, modes, whole, zt, green, hq, hart,
           vb, vl, cosb, sinb, hs, hrow, harv,
           in_sem, out_sem, pot_s, pot_r, w_s, w_r, b_s, b_r, rs_s, rs_r, ag_s, ag_r, hq_s, hq_r, h_s, h_r, g_s, g_r, own_sem, const_sem, tail_s, tail_r, head_s, head_r) = refs
    me = lax.axis_index("slab")
    grp = lax.axis_index("band")
    slab_peers = [(d, lax.rem(me + d, SLABS)) for d in range(1, SLABS)]
    band_peers = [(d, lax.rem(grp + d, GROUPS)) for d in range(1, GROUPS)]

    barrier = pltpu.get_barrier_semaphore()
    for _, q in slab_peers:
        pl.semaphore_signal(barrier, inc=1, device_id={"slab": q}, device_id_type=MESH)
    for _, q in band_peers:
        pl.semaphore_signal(barrier, inc=1, device_id={"band": q}, device_id_type=MESH)

    def load(i):
        at = pl.ds(i * XROWS, XROWS)
        return pltpu.make_async_copy(orb.at[at], ib.at[at], in_sem.at[i])

    def table(i):
        return pltpu.make_async_copy(sources[i], consts[i], const_sem.at[i])

    table(0).start()
    table(1).start()
    for i in range(OWN):
        load(i).start()
    for i in range(2, len(NAMES)):
        table(i).start()
    table(0).wait()
    table(1).wait()

    def slab_copy(src, dst, s, r, q):
        return pltpu.make_async_remote_copy(src, dst, s, r, device_id={"slab": q}, device_id_type=MESH)

    def band_copy(src, dst, s, r, q):
        return pltpu.make_async_remote_copy(src, dst, s, r, device_id={"band": q}, device_id_type=MESH)

    def first(b, carry):
        def local(pair, carry):
            @pl.when(b == 0)
            def _():
                for i in range(2):
                    load(2 * pair + i).wait()

            tiles = [
                jnp.concatenate(
                    [ib[pl.ds((2 * pair + i) * XROWS + 4 * t + b, PAIRS, stride=12), :] for i in range(2)], 0
                )
                for t in range(3)
            ]
            z = []
            for j in range(2):
                x = jnp.concatenate([tiles[j], tiles[j + 1]], 1)
                z.append(times2(x, z_in[pl.ds(256 * j, 256)]))
            x = jnp.concatenate(
                [
                    jnp.concatenate(
                        [z[j][48 * i : 48 * i + 48, 128 * c : 128 * c + 128] for j in range(2) for c in range(2)], 0
                    )
                    for i in range(2)
                ],
                1,
            )
            r = left2(y_in[...], x)
            for i in range(2):
                x = 2 * pair + i
                tiles = packed([r[48 * j : 48 * j + 48, 128 * i : 128 * i + 128] for j in range(4)])
                for t in range(3):
                    for c in range(2):
                        wire[pl.ds(b * BAND + t * 24 + c * OWN + x, 24, stride=72), :] = tiles[t][24 * c : 24 * c + 24]
            return carry

        lax.fori_loop(0, OWN // 2, local, 0)

        @pl.when(b == 0)
        def _():
            pl.semaphore_wait(barrier, SLABS - 1 + GROUPS - 1)

        @pl.when(b < BANDS - 1)
        def _():
            for d, q in slab_peers:
                send_line(b, d, q).start()

        @pl.when(b == BANDS - 1)
        def _():
            for a in range(3):
                for d, q in slab_peers:
                    send_tail(a, d, q).start()

        own_line(b).start()
        return carry

    def send_tail(a, d, q):
        return slab_copy(
            wire.at[pl.ds((BANDS - 1) * BAND + q * BLOCK + 72 * a, 72)],
            lines.at[pl.ds((BANDS - 1) * BAND + me * BLOCK + 72 * a, 72)],
            tail_s.at[a, d],
            tail_r.at[a, d],
            q,
        )

    def send_line(b, d, q):
        return slab_copy(
            wire.at[pl.ds(b * BAND + q * BLOCK, BLOCK)],
            lines.at[pl.ds(b * BAND + me * BLOCK, BLOCK)],
            w_s.at[b, d],
            w_r.at[b, d],
            q,
        )

    def own_line(b):
        at = pl.ds(b * BAND + me * BLOCK, BLOCK)
        return pltpu.make_async_copy(wire.at[at], lines.at[at], own_sem.at[b])

    lax.fori_loop(0, BANDS, first, 0)

    def send_pot(d, q):
        return slab_copy(
            pot.at[:, pl.ds(pl.multiple_of(q * LINE, 128), LINE)], vb.at[me], pot_s.at[d], pot_r.at[d], q
        )

    for d, q in slab_peers:
        send_pot(d, q).start()
    own_pot = pltpu.make_async_copy(
        pot.at[:, pl.ds(pl.multiple_of(me * LINE, 128), LINE)], vb.at[me], own_sem.at[BANDS]
    )
    own_pot.start()

    for i in range(2, len(NAMES)):
        table(i).wait()

    for i in range(8):
        ksq = ky2[...] + kxz[grp, i : i + 1, :]
        zero = ksq == 0.0
        green[:, 128 * i : 128 * i + 128] = jnp.where(zero, 0.0, 4.0 * math.pi / jnp.where(zero, 1.0, ksq))

    dens[...] = jnp.zeros_like(dens)

    def kx_in(b, a):
        x = jnp.concatenate(
            [
                jnp.concatenate(
                    [lines[pl.ds(b * BAND + s * BLOCK + (3 * a + t) * 24, 24)] for s in range(SLABS)], 0
                )
                for t in range(3)
            ],
            1,
        )
        r = left2(x_in[...], x)
        at = pl.ds(pl.multiple_of(a * 384, 128), 384)
        moved[b, :, at] = r
        dens[:, at] += r[:GRID] * r[:GRID] + r[GRID:] * r[GRID:]

    def lines_x(b, carry):
        own_line(b).wait()
        for d, q in slab_peers:
            send_line(b, d, q).wait_recv()

        def chunk(a, carry):
            kx_in(b, a)
            return carry

        lax.fori_loop(0, 3, chunk, 0)
        return carry

    lax.fori_loop(0, BANDS - 1, lines_x, 0)

    def send_part(a, d, q):
        at = pl.ds(pl.multiple_of(a * 384, 128), 384)
        return band_copy(dq.at[pl.ds(pl.multiple_of(q * 8, 8), 8), at], part.at[grp, :, at], rs_s.at[a, d], rs_r.at[a, d], q)

    own_line(BANDS - 1).wait()

    def last_lines(a, carry):
        for d, q in slab_peers:
            send_tail(a, d, q).wait_recv()
        kx_in(BANDS - 1, a)
        at = pl.ds(pl.multiple_of(a * 384, 128), 384)
        dq[:, at] = left(qx[pl.ds(0, 128)], qx[pl.ds(128, 128)], dens[:, at])
        for d, q in band_peers:
            send_part(a, d, q).start()
        return carry

    lax.fori_loop(0, 3, last_lines, 0)

    own_pot.wait()
    for d, q in slab_peers:
        send_pot(d, q).wait_recv()
    for s in range(SLABS):
        vl[OWN * s : OWN * s + OWN, :] = vb[s]

    def send_share(a, d, q):
        at = pl.ds(pl.multiple_of(a * 384, 128), 384)
        return slab_copy(share.at[:, at], whole.at[me, :, at], ag_s.at[a, d], ag_r.at[a, d], q)

    def sums(a, carry):
        at = pl.ds(pl.multiple_of(a * 384, 128), 384)
        for d, q in band_peers:
            send_part(a, d, q).wait_recv()
        total = dq[pl.ds(pl.multiple_of(grp * 8, 8), 8), at]
        for d, q in band_peers:
            total = total + part[q, :, at]
        share[:, at] = total
        for d, q in slab_peers:
            send_share(a, d, q).start()
        whole[me, :, at] = total
        return carry

    lax.fori_loop(0, 3, sums, 0)

    def along_z(a, carry):
        for d, q in slab_peers:
            send_share(a, d, q).wait_recv()
        tiles = [
            jnp.concatenate(
                [whole[s, :, pl.ds(pl.multiple_of(384 * a + 128 * t, 128), 128)] for s in range(SLABS)], 0
            )
            for t in range(3)
        ]
        x = jnp.concatenate(unpacked(tiles), 0)
        zt[pl.ds(pl.multiple_of(256 * a, 256), 256)] = times(x, qz[pl.ds(0, 128)], qz[pl.ds(128, 128)])
        return carry

    lax.fori_loop(0, 3, along_z, 0)
    x = jnp.concatenate([zt[pl.ds(i, GRID, stride=8), :] for i in range(8)], 1)
    x = left(qy[pl.ds(0, GRID)], qy[pl.ds(GRID, GRID)], x) * green[...]
    x = left(qyt[me, 0:16], qyt[me, 16:32], x)
    x = jnp.concatenate([x[:, 128 * i : 128 * i + 128] for i in range(8)], 0)
    zt[pl.ds(0, 128)] = times(x, qzt[pl.ds(0, 128)], qzt[pl.ds(128, 128)])
    for a in range(3):
        tiles = packed([zt[pl.ds(4 * a + j, 8, stride=16), :] for j in range(4)])
        for t in range(3):
            modes[:, 384 * a + 128 * t : 384 * a + 128 * t + 128] = tiles[t]

    def send_modes(d, q):
        return band_copy(modes, hq.at[pl.ds(pl.multiple_of(grp * 8, 8), 8)], hq_s.at[d], hq_r.at[d], q)

    for d, q in band_peers:
        send_modes(d, q).start()
    hq[pl.ds(pl.multiple_of(grp * 8, 8), 8)] = modes[...]
    for d, q in band_peers:
        send_modes(d, q).wait_recv()
    def send_back(b, d, q):
        return slab_copy(
            back.at[pl.ds(b * BAND + q * BLOCK, BLOCK)],
            home.at[pl.ds(b * BAND + me * BLOCK, BLOCK)],
            b_s.at[b, d],
            b_r.at[b, d],
            q,
        )

    def own_back(b):
        at = pl.ds(b * BAND + me * BLOCK, BLOCK)
        return pltpu.make_async_copy(back.at[at], home.at[at], own_sem.at[b])

    def send_head(a, d, q):
        return slab_copy(
            back.at[pl.ds(q * BLOCK + 72 * a, 72)],
            home.at[pl.ds(me * BLOCK + 72 * a, 72)],
            head_s.at[a, d],
            head_r.at[a, d],
            q,
        )

    def kx_out(b, a):
        at = pl.ds(pl.multiple_of(a * 384, 128), 384)
        re = moved[b, 0:GRID, at]
        im = moved[b, GRID : 2 * GRID, at]
        cs = cosb[:, at]
        sn = sinb[:, at]
        x = jnp.concatenate([re * cs + im * sn, im * cs - re * sn], 0)
        r = left2(x_out[...], x)
        for q in range(SLABS):
            for t in range(3):
                back[pl.ds(b * BAND + q * BLOCK + (3 * a + t) * 24, 24)] = r[24 * q : 24 * q + 24, 128 * t : 128 * t + 128]

    def head(a, carry):
        at = pl.ds(pl.multiple_of(a * 384, 128), 384)
        h = left(qxt[pl.ds(0, GRID)], qxt[pl.ds(GRID, GRID)], hq[:, at])
        hart[:, at] = h
        s, c = sin_cos((vl[:, at] + h) * TIME_STEP)
        sinb[:, at] = s * SCALE**6
        cosb[:, at] = c * SCALE**6
        kx_out(0, a)
        for d, q in slab_peers:
            send_head(a, d, q).start()
        return carry

    lax.fori_loop(0, 3, head, 0)
    own_back(0).start()

    for t in range(TILES):
        hs[pl.ds(t, GRID, stride=16), :] = hart[:, 128 * t : 128 * t + 128]

    def send_row(d, q):
        return slab_copy(
            hs.at[pl.ds((q * OWN + grp) * 16, 16)],
            hrow.at[pl.ds((grp * SLABS + me) * 16, 16)],
            h_s.at[d],
            h_r.at[d],
            q,
        )

    own_row = pltpu.make_async_copy(
        hs.at[pl.ds((me * OWN + grp) * 16, 16)], hrow.at[pl.ds((grp * SLABS + me) * 16, 16)], own_sem.at[BANDS]
    )

    def send_rows(d, q, g):
        at = pl.ds(g * (SLABS * 16), SLABS * 16)
        return band_copy(hrow.at[at], hrow.at[at], g_s.at[d], g_r.at[d], q)

    @pl.when(grp < OWN)
    def _():
        own_row.start()
        for d, q in slab_peers:
            send_row(d, q).start()

    def kick(b, carry):
        def chunk(a, carry):
            kx_out(b, a)
            return carry

        lax.fori_loop(0, 3, chunk, 0)
        for d, q in slab_peers:
            send_back(b, d, q).start()
        own_back(b).start()
        return carry

    lax.fori_loop(1, BANDS, kick, 0)

    def store(i):
        at = pl.ds(i * XROWS, XROWS)
        return pltpu.make_async_copy(ob.at[at], ev.at[at], out_sem.at[i])

    def rows_out():
        @pl.when(grp < OWN)
        def _():
            own_row.wait()
            for d, q in slab_peers:
                send_row(d, q).wait_recv()
            for d, q in band_peers:
                send_rows(d, q, grp).start()

    def rows_in():
        for d, _ in band_peers:
            source = lax.rem(grp + GROUPS - d, GROUPS)

            @pl.when(source < OWN)
            def _():
                send_rows(d, source, source).wait_recv()

        for s in range(SLABS):
            for t in range(TILES):
                harv[:, LINE * s + 128 * t : LINE * s + 128 * t + 128] = hrow[
                    pl.ds(16 * s + t, OWN, stride=SLABS * 16), :
                ]
        out_hart.start()

    out_hart = pltpu.make_async_copy(harv, har, own_sem.at[BANDS])

    def last(b, carry):
        @pl.when(b == 1)
        def _():
            rows_out()

        @pl.when(b == 3)
        def _():
            rows_in()

        own_back(b).wait()

        @pl.when(b == 0)
        def _():
            for a in range(3):
                for d, q in slab_peers:
                    send_head(a, d, q).wait_recv()

        @pl.when(b > 0)
        def _():
            for d, q in slab_peers:
                send_back(b, d, q).wait_recv()

        def local(pair, carry):
            cols = []
            for i in range(2):
                x = 2 * pair + i
                tiles = [
                    jnp.concatenate(
                        [home[pl.ds(b * BAND + t * 24 + c * OWN + x, 24, stride=72), :] for c in range(2)], 0
                    )
                    for t in range(3)
                ]
                cols.append(jnp.concatenate(unpacked(tiles), 0))
            r = left2(y_out[...], jnp.concatenate(cols, 1))
            res = []
            for j in range(2):
                x = jnp.concatenate(
                    [
                        jnp.concatenate(
                            [r[96 * j + 48 * c : 96 * j + 48 * c + 48, 128 * i : 128 * i + 128] for c in range(2)], 1
                        )
                        for i in range(2)
                    ],
                    0,
                )
                res.append(times2(x, z_out[pl.ds(256 * j, 256)]))
            tiles = (res[0][:, :128], res[0][:, 128:] + res[1][:, :128], res[1][:, 128:])
            for i in range(2):
                for t in range(3):
                    ob[pl.ds((2 * pair + i) * XROWS + 4 * t + b, PAIRS, stride=12), :] = tiles[t][48 * i : 48 * i + 48]

            @pl.when(b == BANDS - 1)
            def _():
                for i in range(2):
                    store(2 * pair + i).start()

            return carry

        lax.fori_loop(0, OWN // 2, local, 0)
        return carry

    lax.fori_loop(0, BANDS, last, 0)

    @pl.when(grp < OWN)
    def _():
        for d, q in slab_peers:
            send_row(d, q).wait_send()
        for d, q in band_peers:
            send_rows(d, q, grp).wait_send()

    out_hart.wait()
    for d, q in slab_peers:
        send_pot(d, q).wait_send()
        for a in range(3):
            send_share(a, d, q).wait_send()
            send_tail(a, d, q).wait_send()
            send_head(a, d, q).wait_send()
    for d, q in band_peers:
        for a in range(3):
            send_part(a, d, q).wait_send()
        send_modes(d, q).wait_send()

    def drain(b, carry):
        for d, q in slab_peers:
            send_line(b, d, q).wait_send()
            send_back(b + 1, d, q).wait_send()
        return carry

    lax.fori_loop(0, BANDS - 1, drain, 0)
    for i in range(OWN):
        store(i).wait()


def body(orbitals, potential):
    rows = orbitals.reshape(BANDS, OWN, XROWS // BANDS, 128).transpose(1, 2, 0, 3).reshape(OWN * XROWS, 128)
    t = tables()
    consts = [jnp.asarray(t[name]) for name in NAMES]
    vmem = lambda *shape: pltpu.VMEM(shape, F32)
    dma = lambda *shape: pltpu.SemaphoreType.DMA(shape)
    ev, har = pl.pallas_call(
        kernel,
        out_shape=(
            jax.ShapeDtypeStruct((OWN * XROWS, 128), F32),
            jax.ShapeDtypeStruct(potential.shape, F32),
        ),
        in_specs=[pl.BlockSpec(memory_space=pl.ANY)] * (2 + len(consts)),
        out_specs=[pl.BlockSpec(memory_space=pl.ANY)] * 2,
        scratch_shapes=[pltpu.VMEM(c.shape, c.dtype) for c in consts]
        + [
            vmem(OWN * XROWS, 128),
            vmem(BANDS * BAND, 128),
            vmem(BANDS * BAND, 128),
            vmem(BANDS, 2 * GRID, LINE),
            vmem(BANDS * BAND, 128),
            vmem(BANDS * BAND, 128),
            vmem(OWN * XROWS, 128),
            vmem(GRID, LINE),
            vmem(128, LINE),
            vmem(GROUPS, 8, LINE),
            vmem(8, LINE),
            vmem(8, LINE),
            vmem(SLABS, 8, LINE),
            vmem(768, 128),
            vmem(GRID, 1024),
            vmem(128, LINE),
            vmem(GRID, LINE),
            vmem(SLABS, OWN, LINE),
            vmem(GRID, LINE),
            vmem(GRID, LINE),
            vmem(GRID, LINE),
            vmem(GRID * 16, 128),
            vmem(OWN * SLABS * 16, 128),
            vmem(OWN, GRID * GRID),
            dma(OWN), dma(OWN),
            dma(SLABS), dma(SLABS),
            dma(BANDS, SLABS), dma(BANDS, SLABS),
            dma(BANDS, SLABS), dma(BANDS, SLABS),
            dma(3, GROUPS), dma(3, GROUPS),
            dma(3, SLABS), dma(3, SLABS),
            dma(GROUPS), dma(GROUPS),
            dma(SLABS), dma(SLABS),
            dma(GROUPS), dma(GROUPS),
            dma(BANDS + 1),
            dma(len(consts)),
            dma(3, SLABS), dma(3, SLABS),
            dma(3, SLABS), dma(3, SLABS),
        ],
        compiler_params=pltpu.CompilerParams(
            collective_id=0, has_side_effects=True, vmem_limit_bytes=56 * 1024 * 1024
        ),
    )(rows, potential, *consts)
    return ev.reshape(OWN, XROWS // BANDS, BANDS, 128).transpose(2, 0, 1, 3).reshape(orbitals.shape), har


def solution(mesh):
    return jax.shard_map(
        body,
        mesh=mesh,
        in_specs=(P("band", "slab", None), P("slab", None)),
        out_specs=(P("band", "slab", None), P("slab", None)),
        check_vma=False,
    )
```

```python
import functools
import math

import jax
import jax.numpy as jnp
import ml_dtypes
import numpy as np
from jax import lax
from jax.experimental import pallas as pl
from jax.experimental.pallas import tpu as pltpu
from jax.sharding import PartitionSpec as P

GRID = 96
TIME_STEP = 0.1
MESH = pl.DeviceIdType.MESH
SLABS = 8
GROUPS = 16
BANDS = 4
OWN = GRID // SLABS
LINE = OWN * GRID
TILES = LINE // 128
BLOCK = TILES * 2 * OWN
BAND = SLABS * BLOCK
MODES = 56
PIECES = ((0, 24), (24, 16), (40, 16))
XROWS = 2 * GRID * GRID // 128 * BANDS
PAIRS = GRID // 2
SHARE = GRID // GROUPS
SCALE = 1.88474
F32 = jnp.float32
BF16 = jnp.bfloat16


def half_step_line():
    n = np.arange(GRID)
    m = (n + GRID // 2) % GRID - GRID // 2
    k = 2.0 * math.pi / GRID * m
    phase = np.exp(-1j * k * k * TIME_STEP / 4)
    exact = np.fft.ifft(phase) / SCALE
    line = np.stack([exact.real, exact.imag]).astype(np.float32).astype(ml_dtypes.bfloat16).astype(np.float64)

    def worst(values):
        return np.abs(np.fft.fft((values[0] + 1j * values[1]) * SCALE) - phase).max()

    now = worst(line)
    for _ in range(3):
        for part in range(2):
            for t in range(GRID // 2 + 1):
                for sign in (1.0, -1.0):
                    trial = line.copy()
                    step = 2.0 ** (math.floor(math.log2(abs(line[part, t]))) - 7)
                    trial[part, [t, -t % GRID]] = line[part, t] + sign * step
                    error = worst(trial)
                    if error < 0.9999 * now:
                        now, line = error, trial
    return line


def half_step_factor():
    n = np.arange(GRID)
    real, imag = half_step_line()[:, (n[:, None] - n[None, :]) % GRID]
    out = np.zeros((2, GRID, 2, GRID))
    out[0, :, 0] = real
    out[0, :, 1] = -imag
    out[1, :, 0] = imag
    out[1, :, 1] = real
    return out


def real_basis():
    n = np.arange(GRID)
    rows, ksq = [np.full(GRID, 1.0 / math.sqrt(GRID))], [0.0]
    for m in range(1, GRID // 2):
        angle = 2.0 * math.pi * ((m * n) % GRID) / GRID
        rows += [np.cos(angle) * math.sqrt(2.0 / GRID), np.sin(angle) * math.sqrt(2.0 / GRID)]
        ksq += [(2.0 * math.pi * m / GRID) ** 2] * 2
    rows.append(np.where(n % 2 == 0, 1.0, -1.0) / math.sqrt(GRID))
    ksq.append(math.pi**2)
    return np.stack(rows), np.array(ksq)


def exact(matrix):
    return matrix.astype(ml_dtypes.bfloat16)


def split(matrix):
    high = matrix.astype(np.float32).astype(ml_dtypes.bfloat16)
    low = (matrix - high.astype(np.float64)).astype(ml_dtypes.bfloat16)
    return np.stack([high, low])


@functools.lru_cache(maxsize=None)
def tables():
    g = half_step_factor()
    t = {}
    into = g.transpose(2, 3, 0, 1)
    padded = np.zeros((2, GRID, 2, 128))
    padded[..., :GRID] = into
    padded = padded.reshape(2 * GRID, 256)
    za = np.zeros((2, 256, 256))
    za[0, :192] = padded
    za[1, 64:] = padded
    t["z_in"] = exact(za.reshape(512, 256))
    rows = np.zeros((2, 128, 2, GRID))
    rows[:, :GRID] = into
    rows = rows.reshape(256, 2 * GRID)
    zb = np.zeros((2, 256, 256))
    zb[0, :, :192] = rows
    zb[1, :, 64:] = rows
    t["z_out"] = exact(zb.reshape(512, 256))
    j, s, a = np.meshgrid(np.arange(4), np.arange(SLABS), np.arange(3), indexing="ij")
    wire_y = 12 * s + 4 * a + j
    pair_y = 2 * np.arange(PAIRS)[None, :] + np.arange(2)[:, None]
    ky = g[:, wire_y][:, :, :, :, :, pair_y]
    t["y_in"] = exact(ky.transpose(1, 0, 2, 3, 5, 4, 6).reshape(192, 192))
    ky = g[:, pair_y][:, :, :, :, wire_y]
    t["y_out"] = exact(ky.transpose(1, 0, 2, 4, 3, 5, 6).reshape(192, 192))
    kx = g.reshape(2, GRID, 2, SLABS, 3, 4)
    t["x_in"] = exact(kx.transpose(0, 1, 3, 4, 2, 5).reshape(192, 192))
    kx = g.reshape(2, SLABS, 3, 4, 2, GRID)
    t["x_out"] = exact(kx.transpose(1, 2, 0, 3, 4, 5).reshape(192, 192))
    q, ksq = real_basis()
    qx = np.zeros((GROUPS, 8, GRID))
    qx[:, :SHARE] = q.reshape(GROUPS, SHARE, GRID)
    qx = qx.reshape(128, GRID)
    t["qx"] = split(qx * SCALE**6).reshape(256, GRID)
    t["qxt"] = split(qx.T).reshape(192, 128)
    qz = np.zeros((128, 128))
    qz[:GRID, :GRID] = q.T
    t["qz"] = split(qz).reshape(256, 128)
    t["qzt"] = split(qz.T).reshape(256, 128)
    aj_s = 12 * np.arange(SLABS)[None, :] + np.arange(OWN)[:, None]
    t["qy"] = split(q[:, aj_s.reshape(-1)]).reshape(192, GRID)
    qyt = np.zeros((SLABS, 16, GRID))
    qyt[:, :OWN] = q.T.reshape(SLABS, OWN, GRID)
    t["qyt"] = split(qyt).transpose(1, 0, 2, 3).reshape(SLABS, 32, GRID)
    kxz = np.ones((GROUPS, 8, 128))
    kxz[:, :SHARE, :GRID] = ksq.reshape(GROUPS, SHARE)[:, :, None] + ksq[None, None, :]
    t["kxz"] = kxz.astype(np.float32)
    t["ky2"] = np.broadcast_to(ksq[:, None], (GRID, 128)).astype(np.float32)
    return t


NAMES = ("z_in", "y_in", "x_in", "kxz", "ky2", "qx", "qz", "qy", "qyt", "qzt", "qxt", "x_out", "y_out", "z_out")


def halves(x):
    high = x.astype(BF16)
    return high, (x - high.astype(F32)).astype(BF16)


def dot(a, b):
    return jnp.dot(a, b, preferred_element_type=F32)


def times(x, high, low):
    xh, xl = halves(x)
    return dot(xh, high) + (dot(xl, high) + dot(xh, low))


def left(high, low, x):
    xh, xl = halves(x)
    return dot(high, xh) + (dot(high, xl) + dot(low, xh))


def sin_cos(t):
    n = jnp.round(t * (2.0 / math.pi))
    r = t - n * 1.5703125
    r = r - n * 4.8375129699707031e-4
    r = r - n * 7.5495649e-08
    r2 = r * r
    sine = r + r * r2 * (-1.6666654611e-1 + r2 * (8.3321608736e-3 + r2 * -1.9515295891e-4))
    cosine = 1.0 - 0.5 * r2 + r2 * r2 * (4.166664568298827e-2 + r2 * (-1.388731625493765e-3 + r2 * 2.443315711809948e-5))
    quarter = n.astype(jnp.int32) & 3
    odd = (quarter & 1) == 1
    s = jnp.where(odd, cosine, sine)
    c = jnp.where(odd, sine, cosine)
    s = jnp.where(quarter >= 2, -s, s)
    c = jnp.where((quarter == 1) | (quarter == 2), -c, c)
    return s, c


def times2(x, table):
    r = dot(jnp.concatenate(halves(x), 0), table)
    return r[: x.shape[0]] + r[x.shape[0] :]


def left2(table, x):
    r = dot(table, jnp.concatenate(halves(x), 1))
    return r[:, : x.shape[1]] + r[:, x.shape[1] :]


def lane_of(shape):
    return lax.broadcasted_iota(jnp.int32, shape, len(shape) - 1)


def packed(parts):
    lane = lane_of(parts[0].shape)
    r1 = pltpu.roll(parts[1], 96, 1)
    r2 = pltpu.roll(parts[2], 64, 1)
    r3 = pltpu.roll(parts[3], 32, 1)
    return (
        jnp.where(lane < 96, parts[0], r1),
        jnp.where(lane < 64, r1, r2),
        jnp.where(lane < 32, r2, r3),
    )


def unpacked(tiles):
    lane = lane_of(tiles[0].shape)
    return (
        tiles[0],
        pltpu.roll(jnp.where(lane < 64, tiles[1], tiles[0]), 32, 1),
        pltpu.roll(jnp.where(lane < 32, tiles[2], tiles[1]), 64, 1),
        pltpu.roll(tiles[2], 96, 1),
    )


def kernel(orb, pot, *refs):
    sources, refs = refs[: len(NAMES)], refs[len(NAMES) :]
    ev, har, refs = refs[0], refs[1], refs[2:]
    consts, refs = refs[: len(NAMES)], refs[len(NAMES) :]
    z_in, y_in, x_in, kxz, ky2, qx, qz, qy, qyt, qzt, qxt, x_out, y_out, z_out = consts
    (
     ib, wire, lines, moved, back, home, dens, dq, part, share, modes, whole, zt, green, hq, hart,
           vb, vl, cosb, sinb, hs, hrow,
           in_sem, pot_s, pot_r, w_s, w_r, b_s, b_r, rs_s, rs_r, ag_s, ag_r, hq_s, hq_r, h_s, h_r, g_s, g_r, own_sem, const_sem, tail_s, tail_r, head_s, head_r, first_s, first_r, last_s, last_r) = refs
    me = lax.axis_index("slab")
    grp = lax.axis_index("band")
    slab_peers = [(d, lax.rem(me + d, SLABS)) for d in range(1, SLABS)]
    band_peers = [(d, lax.rem(grp + d, GROUPS)) for d in range(1, GROUPS)]

    barrier = pltpu.get_barrier_semaphore()
    for _, q in slab_peers:
        pl.semaphore_signal(barrier, inc=1, device_id={"slab": q}, device_id_type=MESH)
    for _, q in band_peers:
        pl.semaphore_signal(barrier, inc=1, device_id={"band": q}, device_id_type=MESH)

    def load(i):
        at = pl.ds(i * XROWS, XROWS)
        return pltpu.make_async_copy(orb.at[at], ib.at[at], in_sem.at[i])

    def table(i):
        return pltpu.make_async_copy(sources[i], consts[i], const_sem.at[i])

    table(0).start()
    table(1).start()
    for i in range(OWN):
        load(i).start()
    for i in range(2, len(NAMES)):
        table(i).start()
    table(0).wait()
    table(1).wait()

    def slab_copy(src, dst, s, r, q):
        return pltpu.make_async_remote_copy(src, dst, s, r, device_id={"slab": q}, device_id_type=MESH)

    def band_copy(src, dst, s, r, q):
        return pltpu.make_async_remote_copy(src, dst, s, r, device_id={"band": q}, device_id_type=MESH)

    def row_of(pair):
        return pair // 2 * 8 + lax.rem(pair, 2) * 2

    def quad(ref, b, q, k):
        return ref.reshape(BANDS * SLABS * TILES, 24, 128).at[pl.ds((b * SLABS + q) * TILES, TILES), pl.ds(pl.multiple_of(8 * k, 8), 8)]

    def quad_copy(src, dst, b, k, d, q, send, recv):
        return slab_copy(quad(src, b, q, k), quad(dst, b, me, k), send.at[k, d], recv.at[k, d], q)

    def send_first(k, d, q):
        return quad_copy(wire, lines, 0, k, d, q, first_s, first_r)

    def send_last(k, d, q):
        return quad_copy(back, home, BANDS - 1, k, d, q, last_s, last_r)

    def first(b, carry):
        def local(pair, carry):
            @pl.when(b == 0)
            def _():
                for i in range(2):
                    load(2 * pair + i).wait()

            tiles = [
                jnp.concatenate(
                    [ib[pl.ds((2 * pair + i) * XROWS + 4 * t + b, PAIRS, stride=12), :] for i in range(2)], 0
                )
                for t in range(3)
            ]
            z = []
            for j in range(2):
                x = jnp.concatenate([tiles[j], tiles[j + 1]], 1)
                z.append(times2(x, z_in[pl.ds(256 * j, 256)]))
            x = jnp.concatenate(
                [
                    jnp.concatenate(
                        [z[j][48 * i : 48 * i + 48, 128 * c : 128 * c + 128] for j in range(2) for c in range(2)], 0
                    )
                    for i in range(2)
                ],
                1,
            )
            r = left2(y_in[...], x)
            for i in range(2):
                x = 2 * pair + i
                tiles = packed([r[48 * j : 48 * j + 48, 128 * i : 128 * i + 128] for j in range(4)])
                for t in range(3):
                    for c in range(2):
                        wire[pl.ds(b * BAND + t * 24 + 4 * c + row_of(pair) + i, 24, stride=72), :] = tiles[t][24 * c : 24 * c + 24]

            @pl.when((b == 0) & (pair == 1))
            def _():
                pl.semaphore_wait(barrier, SLABS - 1 + GROUPS - 1)

            @pl.when((b == 0) & (lax.rem(pair, 2) == 1))
            def _():
                for d, q in slab_peers:
                    send_first(pair // 2, d, q).start()

            return carry

        lax.fori_loop(0, OWN // 2, local, 0)

        @pl.when((b > 0) & (b < BANDS - 1))
        def _():
            for d, q in slab_peers:
                send_line(b, d, q).start()

        @pl.when(b == BANDS - 1)
        def _():
            for a in range(3):
                for d, q in slab_peers:
                    send_tail(a, d, q).start()

        own_line(b).start()
        return carry

    def send_tail(a, d, q):
        return slab_copy(
            wire.at[pl.ds((BANDS - 1) * BAND + q * BLOCK + 72 * a, 72)],
            lines.at[pl.ds((BANDS - 1) * BAND + me * BLOCK + 72 * a, 72)],
            tail_s.at[a, d],
            tail_r.at[a, d],
            q,
        )

    def send_line(b, d, q):
        return slab_copy(
            wire.at[pl.ds(b * BAND + q * BLOCK, BLOCK)],
            lines.at[pl.ds(b * BAND + me * BLOCK, BLOCK)],
            w_s.at[b, d],
            w_r.at[b, d],
            q,
        )

    def own_line(b):
        at = pl.ds(b * BAND + me * BLOCK, BLOCK)
        return pltpu.make_async_copy(wire.at[at], lines.at[at], own_sem.at[b])

    lax.fori_loop(0, BANDS, first, 0)

    def send_pot(d, q):
        return slab_copy(
            pot.at[:, pl.ds(pl.multiple_of(q * LINE, 128), LINE)], vb.at[me], pot_s.at[d], pot_r.at[d], q
        )

    for d, q in slab_peers:
        send_pot(d, q).start()
    own_pot = pltpu.make_async_copy(
        pot.at[:, pl.ds(pl.multiple_of(me * LINE, 128), LINE)], vb.at[me], own_sem.at[BANDS]
    )
    own_pot.start()

    for i in range(2, len(NAMES)):
        table(i).wait()

    for i in range(8):
        ksq = ky2[...] + kxz[grp, i : i + 1, :]
        zero = ksq == 0.0
        green[:, 128 * i : 128 * i + 128] = jnp.where(zero, 0.0, 4.0 * math.pi / jnp.where(zero, 1.0, ksq))

    dens[...] = jnp.zeros_like(dens)

    def kx_in(b, a):
        x = jnp.concatenate(
            [
                jnp.concatenate(
                    [lines[pl.ds(b * BAND + s * BLOCK + (3 * a + t) * 24, 24)] for s in range(SLABS)], 0
                )
                for t in range(3)
            ],
            1,
        )
        r = left2(x_in[...], x)
        at = pl.ds(pl.multiple_of(a * 384, 128), 384)
        moved[b, :, at] = r
        dens[:, at] += r[:GRID] * r[:GRID] + r[GRID:] * r[GRID:]

    def lines_x(b, carry):
        own_line(b).wait()

        @pl.when(b == 0)
        def _():
            for k in range(3):
                for d, q in slab_peers:
                    send_first(k, d, q).wait_recv()

        @pl.when(b > 0)
        def _():
            for d, q in slab_peers:
                send_line(b, d, q).wait_recv()

        def chunk(a, carry):
            kx_in(b, a)
            return carry

        lax.fori_loop(0, 3, chunk, 0)
        return carry

    lax.fori_loop(0, BANDS - 1, lines_x, 0)

    def send_part(a, d, q):
        at = pl.ds(pl.multiple_of(a * 384, 128), 384)
        return band_copy(dq.at[pl.ds(pl.multiple_of(q * 8, 8), 8), at], part.at[grp, :, at], rs_s.at[a, d], rs_r.at[a, d], q)

    own_line(BANDS - 1).wait()

    def last_lines(a, carry):
        for d, q in slab_peers:
            send_tail(a, d, q).wait_recv()
        kx_in(BANDS - 1, a)
        at = pl.ds(pl.multiple_of(a * 384, 128), 384)
        dq[:, at] = left(qx[pl.ds(0, 128)], qx[pl.ds(128, 128)], dens[:, at])
        for d, q in band_peers:
            send_part(a, d, q).start()
        return carry

    lax.fori_loop(0, 3, last_lines, 0)

    own_pot.wait()
    for d, q in slab_peers:
        send_pot(d, q).wait_recv()
    for s in range(SLABS):
        vl[OWN * s : OWN * s + OWN, :] = vb[s]

    def send_share(a, d, q):
        at = pl.ds(pl.multiple_of(a * 384, 128), 384)
        return slab_copy(share.at[:, at], whole.at[me, :, at], ag_s.at[a, d], ag_r.at[a, d], q)

    def sums(a, carry):
        at = pl.ds(pl.multiple_of(a * 384, 128), 384)
        for d, q in band_peers:
            send_part(a, d, q).wait_recv()
        total = dq[pl.ds(pl.multiple_of(grp * 8, 8), 8), at]
        for d, q in band_peers:
            total = total + part[q, :, at]
        share[:, at] = total
        for d, q in slab_peers:
            send_share(a, d, q).start()
        whole[me, :, at] = total
        return carry

    lax.fori_loop(0, 3, sums, 0)

    def along_z(a, carry):
        for d, q in slab_peers:
            send_share(a, d, q).wait_recv()
        tiles = [
            jnp.concatenate(
                [whole[s, :, pl.ds(pl.multiple_of(384 * a + 128 * t, 128), 128)] for s in range(SLABS)], 0
            )
            for t in range(3)
        ]
        x = jnp.concatenate(unpacked(tiles), 0)
        zt[pl.ds(pl.multiple_of(256 * a, 256), 256)] = times(x, qz[pl.ds(0, 128)], qz[pl.ds(128, 128)])
        return carry

    lax.fori_loop(0, 3, along_z, 0)
    x = jnp.concatenate([zt[pl.ds(i, GRID, stride=8), :] for i in range(8)], 1)
    x = left(qy[pl.ds(0, GRID)], qy[pl.ds(GRID, GRID)], x) * green[...]
    x = left(qyt[me, 0:16], qyt[me, 16:32], x)
    x = jnp.concatenate([x[:, 128 * i : 128 * i + 128] for i in range(8)], 0)
    zt[pl.ds(0, 128)] = times(x, qzt[pl.ds(0, 128)], qzt[pl.ds(128, 128)])
    for a in range(3):
        tiles = packed([zt[pl.ds(4 * a + j, 8, stride=16), :] for j in range(4)])
        for t in range(3):
            modes[SHARE * (3 * a + t) : SHARE * (3 * a + t) + 8, :] = tiles[t]

    def send_modes(k, d, q):
        start, rows = PIECES[k]
        return band_copy(
            modes.at[pl.ds(start, rows)],
            hq.at[pl.ds(grp * MODES + start, rows)],
            hq_s.at[k, d],
            hq_r.at[k, d],
            q,
        )

    for k in range(3):
        for d, q in band_peers:
            send_modes(k, d, q).start()
    hq[pl.ds(pl.multiple_of(grp * MODES, 8), MODES)] = modes[...]

    def send_back(b, d, q):
        return slab_copy(
            back.at[pl.ds(b * BAND + q * BLOCK, BLOCK)],
            home.at[pl.ds(b * BAND + me * BLOCK, BLOCK)],
            b_s.at[b, d],
            b_r.at[b, d],
            q,
        )

    def own_back(b):
        at = pl.ds(b * BAND + me * BLOCK, BLOCK)
        return pltpu.make_async_copy(back.at[at], home.at[at], own_sem.at[b])

    def send_head(a, d, q):
        return slab_copy(
            back.at[pl.ds(q * BLOCK + 72 * a, 72)],
            home.at[pl.ds(me * BLOCK + 72 * a, 72)],
            head_s.at[a, d],
            head_r.at[a, d],
            q,
        )

    def kx_out(b, a):
        at = pl.ds(pl.multiple_of(a * 384, 128), 384)
        re = moved[b, 0:GRID, at]
        im = moved[b, GRID : 2 * GRID, at]
        cs = cosb[:, at]
        sn = sinb[:, at]
        x = jnp.concatenate([re * cs + im * sn, im * cs - re * sn], 0)
        r = left2(x_out[...], x)
        for q in range(SLABS):
            for t in range(3):
                back[pl.ds(b * BAND + q * BLOCK + (3 * a + t) * 24, 24)] = r[24 * q : 24 * q + 24, 128 * t : 128 * t + 128]

    for a in range(3):
        for d, q in band_peers:
            send_modes(a, d, q).wait_recv()
        at = pl.ds(384 * a, 384)
        x = jnp.concatenate(
            [
                jnp.concatenate(
                    [
                        hq[MODES * g + SHARE * (3 * a + t) : MODES * g + SHARE * (3 * a + t) + 8, :]
                        for g in range(GROUPS)
                    ],
                    0,
                )
                for t in range(3)
            ],
            1,
        )
        h = left(qxt[pl.ds(0, GRID)], qxt[pl.ds(GRID, GRID)], x)
        hart[:, at] = h
        s, c = sin_cos((vl[:, at] + h) * TIME_STEP)
        sinb[:, at] = s * SCALE**6
        cosb[:, at] = c * SCALE**6
        kx_out(0, a)
        for d, q in slab_peers:
            send_head(a, d, q).start()
    own_back(0).start()

    for t in range(TILES):
        hs[pl.ds(t, GRID, stride=16), :] = hart[:, 128 * t : 128 * t + 128]

    def send_row(d, q):
        return slab_copy(
            hs.at[pl.ds((q * OWN + grp) * 16, 16)],
            hrow.at[pl.ds((grp * SLABS + me) * 16, 16)],
            h_s.at[d],
            h_r.at[d],
            q,
        )

    own_row = pltpu.make_async_copy(
        hs.at[pl.ds((me * OWN + grp) * 16, 16)], hrow.at[pl.ds((grp * SLABS + me) * 16, 16)], own_sem.at[BANDS]
    )

    def send_rows(d, q, g):
        at = pl.ds(g * (SLABS * 16), SLABS * 16)
        return band_copy(hrow.at[at], hrow.at[at], g_s.at[d], g_r.at[d], q)

    @pl.when(grp < OWN)
    def _():
        own_row.start()
        for d, q in slab_peers:
            send_row(d, q).start()

    def kick(b, carry):
        def chunk(a, carry):
            kx_out(b, a)
            return carry

        lax.fori_loop(0, 3, chunk, 0)
        @pl.when(b < BANDS - 1)
        def _():
            for d, q in slab_peers:
                send_back(b, d, q).start()

        @pl.when(b == BANDS - 1)
        def _():
            for k in range(3):
                for d, q in slab_peers:
                    send_last(k, d, q).start()

        own_back(b).start()
        return carry

    lax.fori_loop(1, BANDS, kick, 0)

    def rows_out():
        @pl.when(grp < OWN)
        def _():
            own_row.wait()
            for d, q in slab_peers:
                send_row(d, q).wait_recv()
            for d, q in band_peers:
                send_rows(d, q, grp).start()

    def rows_in():
        for d, _ in band_peers:
            source = lax.rem(grp + GROUPS - d, GROUPS)

            @pl.when(source < OWN)
            def _():
                send_rows(d, source, source).wait_recv()

        for s in range(SLABS):
            for t in range(TILES):
                har[:, LINE * s + 128 * t : LINE * s + 128 * t + 128] = hrow[
                    pl.ds(16 * s + t, OWN, stride=SLABS * 16), :
                ]

    def last(b, carry):
        @pl.when(b == 1)
        def _():
            rows_out()

        @pl.when(b == 3)
        def _():
            rows_in()

        own_back(b).wait()

        @pl.when(b == 0)
        def _():
            for a in range(3):
                for d, q in slab_peers:
                    send_head(a, d, q).wait_recv()

        @pl.when((b > 0) & (b < BANDS - 1))
        def _():
            for d, q in slab_peers:
                send_back(b, d, q).wait_recv()

        def local(pair, carry):
            @pl.when((b == BANDS - 1) & (lax.rem(pair, 2) == 0))
            def _():
                for d, q in slab_peers:
                    send_last(pair // 2, d, q).wait_recv()

            cols = []
            for i in range(2):
                x = 2 * pair + i
                tiles = [
                    jnp.concatenate(
                        [home[pl.ds(b * BAND + t * 24 + 4 * c + row_of(pair) + i, 24, stride=72), :] for c in range(2)], 0
                    )
                    for t in range(3)
                ]
                cols.append(jnp.concatenate(unpacked(tiles), 0))
            r = left2(y_out[...], jnp.concatenate(cols, 1))
            res = []
            for j in range(2):
                x = jnp.concatenate(
                    [
                        jnp.concatenate(
                            [r[96 * j + 48 * c : 96 * j + 48 * c + 48, 128 * i : 128 * i + 128] for c in range(2)], 1
                        )
                        for i in range(2)
                    ],
                    0,
                )
                res.append(times2(x, z_out[pl.ds(256 * j, 256)]))
            tiles = (res[0][:, :128], res[0][:, 128:] + res[1][:, :128], res[1][:, 128:])
            for i in range(2):
                for t in range(3):
                    ev[pl.ds((2 * pair + i) * XROWS + 4 * t + b, PAIRS, stride=12), :] = tiles[t][48 * i : 48 * i + 48]

            return carry

        lax.fori_loop(0, OWN // 2, local, 0)
        return carry

    lax.fori_loop(0, BANDS, last, 0)

    @pl.when(grp < OWN)
    def _():
        for d, q in slab_peers:
            send_row(d, q).wait_send()
        for d, q in band_peers:
            send_rows(d, q, grp).wait_send()

    for d, q in slab_peers:
        send_pot(d, q).wait_send()
        for a in range(3):
            send_share(a, d, q).wait_send()
            send_tail(a, d, q).wait_send()
            send_head(a, d, q).wait_send()
            send_first(a, d, q).wait_send()
            send_last(a, d, q).wait_send()
    for d, q in band_peers:
        for a in range(3):
            send_part(a, d, q).wait_send()
            send_modes(a, d, q).wait_send()

    def drain(b, carry):
        for d, q in slab_peers:
            send_line(b, d, q).wait_send()
            send_back(b, d, q).wait_send()
        return carry

    lax.fori_loop(1, BANDS - 1, drain, 0)


def result(ev, har, ev_out, har_out, sem):
    n = ev.shape[0] // 8
    copies = [
        pltpu.make_async_copy(ev.at[pl.ds(n * i, n)], ev_out.at[pl.ds(n * i, n)], sem.at[i]) for i in range(8)
    ]
    copies.append(pltpu.make_async_copy(har, har_out, sem.at[8]))
    for copy in copies:
        copy.start()
    for copy in copies:
        copy.wait()


def body(orbitals, potential):
    rows = orbitals.reshape(BANDS, OWN, XROWS // BANDS, 128).transpose(1, 2, 0, 3).reshape(OWN * XROWS, 128)
    t = tables()
    consts = [jnp.asarray(t[name]) for name in NAMES]
    vmem = lambda *shape: pltpu.VMEM(shape, F32)
    dma = lambda *shape: pltpu.SemaphoreType.DMA(shape)
    ev, har = pl.pallas_call(
        kernel,
        out_shape=(
            pltpu.VMEM((OWN * XROWS, 128), F32),
            pltpu.VMEM(potential.shape, F32),
        ),
        in_specs=[pl.BlockSpec(memory_space=pl.ANY)] * (2 + len(consts)),
        out_specs=[pl.BlockSpec(memory_space=pltpu.VMEM)] * 2,
        scratch_shapes=[pltpu.VMEM(c.shape, c.dtype) for c in consts]
        + [
            vmem(OWN * XROWS, 128),
            vmem(BANDS * BAND, 128),
            vmem(BANDS * BAND, 128),
            vmem(BANDS, 2 * GRID, LINE),
            vmem(BANDS * BAND, 128),
            vmem(BANDS * BAND, 128),
            vmem(GRID, LINE),
            vmem(128, LINE),
            vmem(GROUPS, 8, LINE),
            vmem(8, LINE),
            vmem(MODES, 128),
            vmem(SLABS, 8, LINE),
            vmem(768, 128),
            vmem(GRID, 1024),
            vmem(GROUPS * MODES, 128),
            vmem(GRID, LINE),
            vmem(SLABS, OWN, LINE),
            vmem(GRID, LINE),
            vmem(GRID, LINE),
            vmem(GRID, LINE),
            vmem(GRID * 16, 128),
            vmem(OWN * SLABS * 16, 128),
            dma(OWN),
            dma(SLABS), dma(SLABS),
            dma(BANDS, SLABS), dma(BANDS, SLABS),
            dma(BANDS, SLABS), dma(BANDS, SLABS),
            dma(3, GROUPS), dma(3, GROUPS),
            dma(3, SLABS), dma(3, SLABS),
            dma(3, GROUPS), dma(3, GROUPS),
            dma(SLABS), dma(SLABS),
            dma(GROUPS), dma(GROUPS),
            dma(BANDS + 1),
            dma(len(consts)),
            dma(3, SLABS), dma(3, SLABS),
            dma(3, SLABS), dma(3, SLABS),
            dma(3, SLABS), dma(3, SLABS),
            dma(3, SLABS), dma(3, SLABS),
        ],
        compiler_params=pltpu.CompilerParams(
            collective_id=0, has_side_effects=True, vmem_limit_bytes=60416 * 1024
        ),
    )(rows, potential, *consts)
    ev, har = pl.pallas_call(
        result,
        out_shape=(jax.ShapeDtypeStruct(ev.shape, F32), jax.ShapeDtypeStruct(har.shape, F32)),
        in_specs=[pl.BlockSpec(memory_space=pltpu.VMEM)] * 2,
        out_specs=[pl.BlockSpec(memory_space=pl.ANY)] * 2,
        scratch_shapes=[pltpu.SemaphoreType.DMA((9,))],
        compiler_params=pltpu.CompilerParams(vmem_limit_bytes=1024 * 1024),
    )(ev, har)
    return ev.reshape(OWN, XROWS // BANDS, BANDS, 128).transpose(2, 0, 1, 3).reshape(orbitals.shape), har


def solution(mesh):
    return jax.shard_map(
        body,
        mesh=mesh,
        in_specs=(P("band", "slab", None), P("slab", None)),
        out_specs=(P("band", "slab", None), P("slab", None)),
        check_vma=False,
    )
```

```python
import functools
import math

import jax
import jax.numpy as jnp
import ml_dtypes
import numpy as np
from jax import lax
from jax.experimental import pallas as pl
from jax.experimental.pallas import tpu as pltpu
from jax.sharding import PartitionSpec as P

GRID = 96
TIME_STEP = 0.1
MESH = pl.DeviceIdType.MESH
SLABS = 8
GROUPS = 16
BANDS = 4
OWN = GRID // SLABS
LINE = OWN * GRID
TILES = LINE // 128
BLOCK = TILES * 2 * OWN
BAND = SLABS * BLOCK
MODES = 56
PIECES = ((0, 24), (24, 16), (40, 16))
XROWS = 2 * GRID * GRID // 128 * BANDS
PAIRS = GRID // 2
SHARE = GRID // GROUPS
SCALE = 1.88474
F32 = jnp.float32
BF16 = jnp.bfloat16


def half_step_line():
    n = np.arange(GRID)
    m = (n + GRID // 2) % GRID - GRID // 2
    k = 2.0 * math.pi / GRID * m
    phase = np.exp(-1j * k * k * TIME_STEP / 4)
    exact = np.fft.ifft(phase) / SCALE
    line = np.stack([exact.real, exact.imag]).astype(np.float32).astype(ml_dtypes.bfloat16).astype(np.float64)

    def worst(values):
        return np.abs(np.fft.fft((values[0] + 1j * values[1]) * SCALE) - phase).max()

    now = worst(line)
    for _ in range(3):
        for part in range(2):
            for t in range(GRID // 2 + 1):
                for sign in (1.0, -1.0):
                    trial = line.copy()
                    step = 2.0 ** (math.floor(math.log2(abs(line[part, t]))) - 7)
                    trial[part, [t, -t % GRID]] = line[part, t] + sign * step
                    error = worst(trial)
                    if error < 0.9999 * now:
                        now, line = error, trial
    return line


def half_step_factor():
    n = np.arange(GRID)
    real, imag = half_step_line()[:, (n[:, None] - n[None, :]) % GRID]
    out = np.zeros((2, GRID, 2, GRID))
    out[0, :, 0] = real
    out[0, :, 1] = -imag
    out[1, :, 0] = imag
    out[1, :, 1] = real
    return out


def real_basis():
    n = np.arange(GRID)
    rows, ksq = [np.full(GRID, 1.0 / math.sqrt(GRID))], [0.0]
    for m in range(1, GRID // 2):
        angle = 2.0 * math.pi * ((m * n) % GRID) / GRID
        rows += [np.cos(angle) * math.sqrt(2.0 / GRID), np.sin(angle) * math.sqrt(2.0 / GRID)]
        ksq += [(2.0 * math.pi * m / GRID) ** 2] * 2
    rows.append(np.where(n % 2 == 0, 1.0, -1.0) / math.sqrt(GRID))
    ksq.append(math.pi**2)
    return np.stack(rows), np.array(ksq)


def exact(matrix):
    return matrix.astype(ml_dtypes.bfloat16)


def split(matrix):
    high = matrix.astype(np.float32).astype(ml_dtypes.bfloat16)
    low = (matrix - high.astype(np.float64)).astype(ml_dtypes.bfloat16)
    return np.stack([high, low])


@functools.lru_cache(maxsize=None)
def tables():
    g = half_step_factor()
    t = {}
    into = g.transpose(2, 3, 0, 1)
    padded = np.zeros((2, GRID, 2, 128))
    padded[..., :GRID] = into
    padded = padded.reshape(2 * GRID, 256)
    za = np.zeros((2, 256, 256))
    za[0, :192] = padded
    za[1, 64:] = padded
    t["z_in"] = exact(za.reshape(512, 256))
    rows = np.zeros((2, 128, 2, GRID))
    rows[:, :GRID] = into
    rows = rows.reshape(256, 2 * GRID)
    zb = np.zeros((2, 256, 256))
    zb[0, :, :192] = rows
    zb[1, :, 64:] = rows
    t["z_out"] = exact(zb.reshape(512, 256))
    j, s, a = np.meshgrid(np.arange(4), np.arange(SLABS), np.arange(3), indexing="ij")
    wire_y = 12 * s + 4 * a + j
    pair_y = 2 * np.arange(PAIRS)[None, :] + np.arange(2)[:, None]
    ky = g[:, wire_y][:, :, :, :, :, pair_y]
    t["y_in"] = exact(ky.transpose(1, 0, 2, 3, 5, 4, 6).reshape(192, 192))
    ky = g[:, pair_y][:, :, :, :, wire_y]
    t["y_out"] = exact(ky.transpose(1, 0, 2, 4, 3, 5, 6).reshape(192, 192))
    kx = g.reshape(2, GRID, 2, SLABS, 3, 4)
    t["x_in"] = exact(kx.transpose(0, 1, 3, 4, 2, 5).reshape(192, 192))
    kx = g.reshape(2, SLABS, 3, 4, 2, GRID)
    t["x_out"] = exact(kx.transpose(1, 2, 0, 3, 4, 5).reshape(192, 192))
    q, ksq = real_basis()
    qx = np.zeros((GROUPS, 8, GRID))
    qx[:, :SHARE] = q.reshape(GROUPS, SHARE, GRID)
    qx = qx.reshape(128, GRID)
    t["qx"] = split(qx * SCALE**6).reshape(256, GRID)
    t["qxt"] = split(qx.T).reshape(192, 128)
    qz = np.zeros((128, 128))
    qz[:GRID, :GRID] = q.T
    t["qz"] = split(qz).reshape(256, 128)
    t["qzt"] = split(qz.T).reshape(256, 128)
    aj_s = 12 * np.arange(SLABS)[None, :] + np.arange(OWN)[:, None]
    t["qy"] = split(q[:, aj_s.reshape(-1)]).reshape(192, GRID)
    qyt = np.zeros((SLABS, 16, GRID))
    qyt[:, :OWN] = q.T.reshape(SLABS, OWN, GRID)
    t["qyt"] = split(qyt).transpose(1, 0, 2, 3).reshape(SLABS, 32, GRID)
    kxz = np.ones((GROUPS, 8, 128))
    kxz[:, :SHARE, :GRID] = ksq.reshape(GROUPS, SHARE)[:, :, None] + ksq[None, None, :]
    t["kxz"] = kxz.astype(np.float32)
    t["ky2"] = np.broadcast_to(ksq[:, None], (GRID, 128)).astype(np.float32)
    return t


NAMES = ("z_in", "y_in", "x_in", "kxz", "ky2", "qx", "qz", "qy", "qyt", "qzt", "qxt", "x_out", "y_out", "z_out")


def halves(x):
    high = x.astype(BF16)
    return high, (x - high.astype(F32)).astype(BF16)


def dot(a, b):
    return jnp.dot(a, b, preferred_element_type=F32)


def times(x, high, low):
    xh, xl = halves(x)
    return dot(xh, high) + (dot(xl, high) + dot(xh, low))


def left(high, low, x):
    xh, xl = halves(x)
    return dot(high, xh) + (dot(high, xl) + dot(low, xh))


def sin_cos(t):
    n = jnp.round(t * (2.0 / math.pi))
    r = t - n * 1.5703125
    r = r - n * 4.8375129699707031e-4
    r = r - n * 7.5495649e-08
    r2 = r * r
    sine = r + r * r2 * (-1.6666654611e-1 + r2 * (8.3321608736e-3 + r2 * -1.9515295891e-4))
    cosine = 1.0 - 0.5 * r2 + r2 * r2 * (4.166664568298827e-2 + r2 * (-1.388731625493765e-3 + r2 * 2.443315711809948e-5))
    quarter = n.astype(jnp.int32) & 3
    odd = (quarter & 1) == 1
    s = jnp.where(odd, cosine, sine)
    c = jnp.where(odd, sine, cosine)
    s = jnp.where(quarter >= 2, -s, s)
    c = jnp.where((quarter == 1) | (quarter == 2), -c, c)
    return s, c


def times2(x, table):
    r = dot(jnp.concatenate(halves(x), 0), table)
    return r[: x.shape[0]] + r[x.shape[0] :]


def left2(table, x):
    r = dot(table, jnp.concatenate(halves(x), 1))
    return r[:, : x.shape[1]] + r[:, x.shape[1] :]


def lane_of(shape):
    return lax.broadcasted_iota(jnp.int32, shape, len(shape) - 1)


def packed(parts):
    lane = lane_of(parts[0].shape)
    r1 = pltpu.roll(parts[1], 96, 1)
    r2 = pltpu.roll(parts[2], 64, 1)
    r3 = pltpu.roll(parts[3], 32, 1)
    return (
        jnp.where(lane < 96, parts[0], r1),
        jnp.where(lane < 64, r1, r2),
        jnp.where(lane < 32, r2, r3),
    )


def unpacked(tiles):
    lane = lane_of(tiles[0].shape)
    return (
        tiles[0],
        pltpu.roll(jnp.where(lane < 64, tiles[1], tiles[0]), 32, 1),
        pltpu.roll(jnp.where(lane < 32, tiles[2], tiles[1]), 64, 1),
        pltpu.roll(tiles[2], 96, 1),
    )


def kernel(orb, pot, *refs):
    sources, refs = refs[: len(NAMES)], refs[len(NAMES) :]
    ev, har, refs = refs[0], refs[1], refs[2:]
    consts, refs = refs[: len(NAMES)], refs[len(NAMES) :]
    z_in, y_in, x_in, kxz, ky2, qx, qz, qy, qyt, qzt, qxt, x_out, y_out, z_out = consts
    (
     ib, wire, lines, moved, back, home, dens, dq, part, share, modes, whole, zt, green, hq, hart,
           vb, vl, cosb, sinb, hs, hrow,
           in_sem, pot_s, pot_r, w_s, w_r, b_s, b_r, rs_s, rs_r, ag_s, ag_r, hq_s, hq_r, h_s, h_r, g_s, g_r, own_sem, const_sem, tail_s, tail_r, head_s, head_r, first_s, first_r, last_s, last_r) = refs
    me = lax.axis_index("slab")
    grp = lax.axis_index("band")
    slab_peers = [(d, lax.rem(me + d, SLABS)) for d in range(1, SLABS)]
    band_peers = [(d, lax.rem(grp + d, GROUPS)) for d in range(1, GROUPS)]

    barrier = pltpu.get_barrier_semaphore()
    for _, q in slab_peers:
        pl.semaphore_signal(barrier, inc=1, device_id={"slab": q}, device_id_type=MESH)
    for _, q in band_peers:
        pl.semaphore_signal(barrier, inc=1, device_id={"band": q}, device_id_type=MESH)

    def load(i):
        at = pl.ds(i * 2 * XROWS, 2 * XROWS)
        return pltpu.make_async_copy(orb.at[at], ib.at[at], in_sem.at[i])

    def table(i):
        return pltpu.make_async_copy(sources[i], consts[i], const_sem.at[i])

    table(0).start()
    table(1).start()
    for i in range(OWN // 2):
        load(i).start()
    for i in range(2, len(NAMES)):
        table(i).start()
    table(0).wait()
    table(1).wait()

    def slab_copy(src, dst, s, r, q):
        return pltpu.make_async_remote_copy(src, dst, s, r, device_id={"slab": q}, device_id_type=MESH)

    def band_copy(src, dst, s, r, q):
        return pltpu.make_async_remote_copy(src, dst, s, r, device_id={"band": q}, device_id_type=MESH)

    def row_of(pair):
        return pair // 2 * 8 + lax.rem(pair, 2) * 2

    def quad(ref, b, q, k):
        return ref.reshape(BANDS * SLABS * TILES, 24, 128).at[pl.ds((b * SLABS + q) * TILES, TILES), pl.ds(pl.multiple_of(8 * k, 8), 8)]

    def quad_copy(src, dst, b, k, d, q, send, recv):
        return slab_copy(quad(src, b, q, k), quad(dst, b, me, k), send.at[k], recv.at[k], q)

    def send_first(k, d, q):
        return quad_copy(wire, lines, 0, k, d, q, first_s, first_r)

    def send_last(k, d, q):
        return quad_copy(back, home, BANDS - 1, k, d, q, last_s, last_r)

    def done(view, sem):
        pltpu.make_async_copy(view, view, sem).wait()

    def rows(ref, n):
        return ref.at[pl.ds(0, n)]

    OTHERS, REST = SLABS - 1, GROUPS - 1

    def first(b, carry):
        def local(pair, carry):
            @pl.when(b == 0)
            def _():
                load(pair).wait()

            tiles = [
                jnp.concatenate(
                    [ib[pl.ds((2 * pair + i) * XROWS + 4 * t + b, PAIRS, stride=12), :] for i in range(2)], 0
                )
                for t in range(3)
            ]
            z = []
            for j in range(2):
                x = jnp.concatenate([tiles[j], tiles[j + 1]], 1)
                z.append(times2(x, z_in[pl.ds(256 * j, 256)]))
            x = jnp.concatenate(
                [
                    jnp.concatenate(
                        [z[j][48 * i : 48 * i + 48, 128 * c : 128 * c + 128] for j in range(2) for c in range(2)], 0
                    )
                    for i in range(2)
                ],
                1,
            )
            r = left2(y_in[...], x)
            for i in range(2):
                x = 2 * pair + i
                tiles = packed([r[48 * j : 48 * j + 48, 128 * i : 128 * i + 128] for j in range(4)])
                for t in range(3):
                    for c in range(2):
                        wire[pl.ds(b * BAND + t * 24 + 4 * c + row_of(pair) + i, 24, stride=72), :] = tiles[t][24 * c : 24 * c + 24]

            @pl.when((b == 0) & (pair == 1))
            def _():
                pl.semaphore_wait(barrier, SLABS - 1 + GROUPS - 1)

            @pl.when((b == 0) & (lax.rem(pair, 2) == 1))
            def _():
                for d, q in slab_peers:
                    send_first(pair // 2, d, q).start()

            return carry

        lax.fori_loop(0, OWN // 2, local, 0)

        @pl.when((b > 0) & (b < BANDS - 1))
        def _():
            for d, q in slab_peers:
                send_line(b, d, q).start()

        @pl.when(b == BANDS - 1)
        def _():
            for a in range(3):
                for d, q in slab_peers:
                    send_tail(a, d, q).start()

        own_line(b).start()
        return carry

    def send_tail(a, d, q):
        return slab_copy(
            wire.at[pl.ds((BANDS - 1) * BAND + q * BLOCK + 72 * a, 72)],
            lines.at[pl.ds((BANDS - 1) * BAND + me * BLOCK + 72 * a, 72)],
            tail_s.at[a],
            tail_r.at[a],
            q,
        )

    def send_line(b, d, q):
        return slab_copy(
            wire.at[pl.ds(b * BAND + q * BLOCK, BLOCK)],
            lines.at[pl.ds(b * BAND + me * BLOCK, BLOCK)],
            w_s.at[b],
            w_r.at[b],
            q,
        )

    def own_line(b):
        at = pl.ds(b * BAND + me * BLOCK, BLOCK)
        return pltpu.make_async_copy(wire.at[at], lines.at[at], own_sem.at[b])

    lax.fori_loop(0, BANDS, first, 0)

    def send_pot(d, q):
        return slab_copy(
            pot.at[:, pl.ds(pl.multiple_of(q * LINE, 128), LINE)], vb.at[me], pot_s.at[0], pot_r.at[0], q
        )

    for d, q in slab_peers:
        send_pot(d, q).start()
    own_pot = pltpu.make_async_copy(
        pot.at[:, pl.ds(pl.multiple_of(me * LINE, 128), LINE)], vb.at[me], own_sem.at[BANDS]
    )
    own_pot.start()

    for i in range(2, len(NAMES)):
        table(i).wait()

    for i in range(8):
        ksq = ky2[...] + kxz[grp, i : i + 1, :]
        zero = ksq == 0.0
        green[:, 128 * i : 128 * i + 128] = jnp.where(zero, 0.0, 4.0 * math.pi / jnp.where(zero, 1.0, ksq))

    dens[...] = jnp.zeros_like(dens)

    def kx_in(b, a):
        x = jnp.concatenate(
            [
                jnp.concatenate(
                    [lines[pl.ds(b * BAND + s * BLOCK + (3 * a + t) * 24, 24)] for s in range(SLABS)], 0
                )
                for t in range(3)
            ],
            1,
        )
        r = left2(x_in[...], x)
        at = pl.ds(pl.multiple_of(a * 384, 128), 384)
        moved[b, :, at] = r
        dens[:, at] += r[:GRID] * r[:GRID] + r[GRID:] * r[GRID:]

    def lines_x(b, carry):
        own_line(b).wait()

        @pl.when(b == 0)
        def _():
            for k in range(3):
                done(rows(lines, OTHERS * 72), first_r.at[k])

        @pl.when(b > 0)
        def _():
            done(rows(lines, OTHERS * BLOCK), w_r.at[b])

        def chunk(a, carry):
            kx_in(b, a)
            return carry

        lax.fori_loop(0, 3, chunk, 0)
        return carry

    lax.fori_loop(0, BANDS - 1, lines_x, 0)

    def send_part(a, d, q):
        at = pl.ds(pl.multiple_of(a * 384, 128), 384)
        return band_copy(dq.at[pl.ds(pl.multiple_of(q * 8, 8), 8), at], part.at[grp, :, at], rs_s.at[a], rs_r.at[a], q)

    own_line(BANDS - 1).wait()

    def last_lines(a, carry):
        done(rows(lines, OTHERS * 72), tail_r.at[a])
        kx_in(BANDS - 1, a)
        at = pl.ds(pl.multiple_of(a * 384, 128), 384)
        dq[:, at] = left(qx[pl.ds(0, 128)], qx[pl.ds(128, 128)], dens[:, at])
        for d, q in band_peers:
            send_part(a, d, q).start()
        return carry

    lax.fori_loop(0, 3, last_lines, 0)

    own_pot.wait()
    done(rows(vb, OTHERS), pot_r.at[0])
    for s in range(SLABS):
        vl[OWN * s : OWN * s + OWN, :] = vb[s]

    def send_share(a, d, q):
        at = pl.ds(pl.multiple_of(a * 384, 128), 384)
        return slab_copy(share.at[:, at], whole.at[me, :, at], ag_s.at[a], ag_r.at[a], q)

    def sums(a, carry):
        at = pl.ds(pl.multiple_of(a * 384, 128), 384)
        done(part.at[pl.ds(0, REST), :, at], rs_r.at[a])
        total = dq[pl.ds(pl.multiple_of(grp * 8, 8), 8), at]
        for d, q in band_peers:
            total = total + part[q, :, at]
        share[:, at] = total
        for d, q in slab_peers:
            send_share(a, d, q).start()
        whole[me, :, at] = total
        return carry

    lax.fori_loop(0, 3, sums, 0)

    def along_z(a, carry):
        done(whole.at[pl.ds(0, OTHERS), :, pl.ds(pl.multiple_of(a * 384, 128), 384)], ag_r.at[a])
        tiles = [
            jnp.concatenate(
                [whole[s, :, pl.ds(pl.multiple_of(384 * a + 128 * t, 128), 128)] for s in range(SLABS)], 0
            )
            for t in range(3)
        ]
        x = jnp.concatenate(unpacked(tiles), 0)
        zt[pl.ds(pl.multiple_of(256 * a, 256), 256)] = times(x, qz[pl.ds(0, 128)], qz[pl.ds(128, 128)])
        return carry

    lax.fori_loop(0, 3, along_z, 0)
    x = jnp.concatenate([zt[pl.ds(i, GRID, stride=8), :] for i in range(8)], 1)
    x = left(qy[pl.ds(0, GRID)], qy[pl.ds(GRID, GRID)], x) * green[...]
    x = left(qyt[me, 0:16], qyt[me, 16:32], x)
    x = jnp.concatenate([x[:, 128 * i : 128 * i + 128] for i in range(8)], 0)
    zt[pl.ds(0, 128)] = times(x, qzt[pl.ds(0, 128)], qzt[pl.ds(128, 128)])
    for a in range(3):
        tiles = packed([zt[pl.ds(4 * a + j, 8, stride=16), :] for j in range(4)])
        for t in range(3):
            modes[SHARE * (3 * a + t) : SHARE * (3 * a + t) + 8, :] = tiles[t]

    def send_modes(k, d, q):
        start, rows = PIECES[k]
        return band_copy(
            modes.at[pl.ds(start, rows)],
            hq.at[pl.ds(grp * MODES + start, rows)],
            hq_s.at[k],
            hq_r.at[k],
            q,
        )

    for k in range(3):
        for d, q in band_peers:
            send_modes(k, d, q).start()
    hq[pl.ds(pl.multiple_of(grp * MODES, 8), MODES)] = modes[...]

    def send_back(b, d, q):
        return slab_copy(
            back.at[pl.ds(b * BAND + q * BLOCK, BLOCK)],
            home.at[pl.ds(b * BAND + me * BLOCK, BLOCK)],
            b_s.at[b],
            b_r.at[b],
            q,
        )

    def own_back(b):
        at = pl.ds(b * BAND + me * BLOCK, BLOCK)
        return pltpu.make_async_copy(back.at[at], home.at[at], own_sem.at[b])

    def send_head(a, d, q):
        return slab_copy(
            back.at[pl.ds(q * BLOCK + 72 * a, 72)],
            home.at[pl.ds(me * BLOCK + 72 * a, 72)],
            head_s.at[a],
            head_r.at[a],
            q,
        )

    def kx_out(b, a):
        at = pl.ds(pl.multiple_of(a * 384, 128), 384)
        re = moved[b, 0:GRID, at]
        im = moved[b, GRID : 2 * GRID, at]
        cs = cosb[:, at]
        sn = sinb[:, at]
        x = jnp.concatenate([re * cs + im * sn, im * cs - re * sn], 0)
        r = left2(x_out[...], x)
        for q in range(SLABS):
            for t in range(3):
                back[pl.ds(b * BAND + q * BLOCK + (3 * a + t) * 24, 24)] = r[24 * q : 24 * q + 24, 128 * t : 128 * t + 128]

    for a in range(3):
        done(rows(hq, REST * PIECES[a][1]), hq_r.at[a])
        at = pl.ds(384 * a, 384)
        x = jnp.concatenate(
            [
                jnp.concatenate(
                    [
                        hq[MODES * g + SHARE * (3 * a + t) : MODES * g + SHARE * (3 * a + t) + 8, :]
                        for g in range(GROUPS)
                    ],
                    0,
                )
                for t in range(3)
            ],
            1,
        )
        h = left(qxt[pl.ds(0, GRID)], qxt[pl.ds(GRID, GRID)], x)
        hart[:, at] = h
        s, c = sin_cos((vl[:, at] + h) * TIME_STEP)
        sinb[:, at] = s * SCALE**6
        cosb[:, at] = c * SCALE**6
        kx_out(0, a)
        for d, q in slab_peers:
            send_head(a, d, q).start()
    own_back(0).start()

    for t in range(TILES):
        hs[pl.ds(t, GRID, stride=16), :] = hart[:, 128 * t : 128 * t + 128]

    def send_row(d, q):
        return slab_copy(
            hs.at[pl.ds((q * OWN + grp) * 16, 16)],
            hrow.at[pl.ds((grp * SLABS + me) * 16, 16)],
            h_s.at[0],
            h_r.at[0],
            q,
        )

    own_row = pltpu.make_async_copy(
        hs.at[pl.ds((me * OWN + grp) * 16, 16)], hrow.at[pl.ds((grp * SLABS + me) * 16, 16)], own_sem.at[BANDS]
    )

    def send_rows(d, q, g):
        at = pl.ds(g * (SLABS * 16), SLABS * 16)
        return band_copy(hrow.at[at], hrow.at[at], g_s.at[0], g_r.at[0], q)

    @pl.when(grp < OWN)
    def _():
        own_row.start()
        for d, q in slab_peers:
            send_row(d, q).start()

    def kick(b, carry):
        def chunk(a, carry):
            kx_out(b, a)
            return carry

        lax.fori_loop(0, 3, chunk, 0)
        @pl.when(b < BANDS - 1)
        def _():
            for d, q in slab_peers:
                send_back(b, d, q).start()

        @pl.when(b == BANDS - 1)
        def _():
            for k in range(3):
                for d, q in slab_peers:
                    send_last(k, d, q).start()

        own_back(b).start()
        return carry

    lax.fori_loop(1, BANDS, kick, 0)

    def rows_out():
        @pl.when(grp < OWN)
        def _():
            own_row.wait()
            done(rows(hrow, OTHERS * 16), h_r.at[0])
            for d, q in band_peers:
                send_rows(d, q, grp).start()

    def rows_in():
        @pl.when(grp < OWN)
        def _():
            done(rows(hrow, (OWN - 1) * SLABS * 16), g_r.at[0])

        @pl.when(grp >= OWN)
        def _():
            done(rows(hrow, OWN * SLABS * 16), g_r.at[0])

        for s in range(SLABS):
            for t in range(TILES):
                har[:, LINE * s + 128 * t : LINE * s + 128 * t + 128] = hrow[
                    pl.ds(16 * s + t, OWN, stride=SLABS * 16), :
                ]

    def last(b, carry):
        @pl.when(b == 1)
        def _():
            rows_out()

        @pl.when(b == 3)
        def _():
            rows_in()

        own_back(b).wait()

        @pl.when(b == 0)
        def _():
            for a in range(3):
                done(rows(home, OTHERS * 72), head_r.at[a])

        @pl.when((b > 0) & (b < BANDS - 1))
        def _():
            done(rows(home, OTHERS * BLOCK), b_r.at[b])

        def local(pair, carry):
            @pl.when((b == BANDS - 1) & (lax.rem(pair, 2) == 0))
            def _():
                done(rows(home, OTHERS * 72), last_r.at[pair // 2])

            cols = []
            for i in range(2):
                x = 2 * pair + i
                tiles = [
                    jnp.concatenate(
                        [home[pl.ds(b * BAND + t * 24 + 4 * c + row_of(pair) + i, 24, stride=72), :] for c in range(2)], 0
                    )
                    for t in range(3)
                ]
                cols.append(jnp.concatenate(unpacked(tiles), 0))
            r = left2(y_out[...], jnp.concatenate(cols, 1))
            res = []
            for j in range(2):
                x = jnp.concatenate(
                    [
                        jnp.concatenate(
                            [r[96 * j + 48 * c : 96 * j + 48 * c + 48, 128 * i : 128 * i + 128] for c in range(2)], 1
                        )
                        for i in range(2)
                    ],
                    0,
                )
                res.append(times2(x, z_out[pl.ds(256 * j, 256)]))
            tiles = (res[0][:, :128], res[0][:, 128:] + res[1][:, :128], res[1][:, 128:])
            for i in range(2):
                for t in range(3):
                    ev[pl.ds((2 * pair + i) * XROWS + 4 * t + b, PAIRS, stride=12), :] = tiles[t][48 * i : 48 * i + 48]

            return carry

        lax.fori_loop(0, OWN // 2, local, 0)
        return carry

    lax.fori_loop(0, BANDS, last, 0)

    @pl.when(grp < OWN)
    def _():
        done(rows(hs, OTHERS * 16), h_s.at[0])
        done(rows(wire, REST * SLABS * 16), g_s.at[0])

    done(rows(vb, OTHERS), pot_s.at[0])
    for a in range(3):
        done(whole.at[pl.ds(0, OTHERS), :, pl.ds(384 * a, 384)], ag_s.at[a])
        done(part.at[pl.ds(0, REST), :, pl.ds(384 * a, 384)], rs_s.at[a])
        done(rows(hq, REST * PIECES[a][1]), hq_s.at[a])
        done(rows(wire, OTHERS * 72), first_s.at[a])
        done(rows(wire, OTHERS * 72), tail_s.at[a])
        done(rows(back, OTHERS * 72), head_s.at[a])
        done(rows(back, OTHERS * 72), last_s.at[a])
    for b in range(1, BANDS - 1):
        done(rows(wire, OTHERS * BLOCK), w_s.at[b])
        done(rows(back, OTHERS * BLOCK), b_s.at[b])


def result(ev, har, ev_out, har_out, sem):
    n = ev.shape[0] // 8
    copies = [
        pltpu.make_async_copy(ev.at[pl.ds(n * i, n)], ev_out.at[pl.ds(n * i, n)], sem.at[i]) for i in range(8)
    ]
    copies.append(pltpu.make_async_copy(har, har_out, sem.at[8]))
    for copy in copies:
        copy.start()
    for copy in copies:
        copy.wait()


def body(orbitals, potential):
    rows = orbitals.reshape(BANDS, OWN, XROWS // BANDS, 128).transpose(1, 2, 0, 3).reshape(OWN * XROWS, 128)
    t = tables()
    consts = [jnp.asarray(t[name]) for name in NAMES]
    vmem = lambda *shape: pltpu.VMEM(shape, F32)
    dma = lambda *shape: pltpu.SemaphoreType.DMA(shape)
    ev, har = pl.pallas_call(
        kernel,
        out_shape=(
            pltpu.VMEM((OWN * XROWS, 128), F32),
            pltpu.VMEM(potential.shape, F32),
        ),
        in_specs=[pl.BlockSpec(memory_space=pl.ANY)] * (2 + len(consts)),
        out_specs=[pl.BlockSpec(memory_space=pltpu.VMEM)] * 2,
        scratch_shapes=[pltpu.VMEM(c.shape, c.dtype) for c in consts]
        + [
            vmem(OWN * XROWS, 128),
            vmem(BANDS * BAND, 128),
            vmem(BANDS * BAND, 128),
            vmem(BANDS, 2 * GRID, LINE),
            vmem(BANDS * BAND, 128),
            vmem(BANDS * BAND, 128),
            vmem(GRID, LINE),
            vmem(128, LINE),
            vmem(GROUPS, 8, LINE),
            vmem(8, LINE),
            vmem(MODES, 128),
            vmem(SLABS, 8, LINE),
            vmem(768, 128),
            vmem(GRID, 1024),
            vmem(GROUPS * MODES, 128),
            vmem(GRID, LINE),
            vmem(SLABS, OWN, LINE),
            vmem(GRID, LINE),
            vmem(GRID, LINE),
            vmem(GRID, LINE),
            vmem(GRID * 16, 128),
            vmem(OWN * SLABS * 16, 128),
            dma(OWN // 2),
            dma(1), dma(1),
            dma(BANDS), dma(BANDS),
            dma(BANDS), dma(BANDS),
            dma(3), dma(3),
            dma(3), dma(3),
            dma(3), dma(3),
            dma(1), dma(1),
            dma(1), dma(1),
            dma(BANDS + 1),
            dma(len(consts)),
            dma(3), dma(3),
            dma(3), dma(3),
            dma(3), dma(3),
            dma(3), dma(3),
        ],
        compiler_params=pltpu.CompilerParams(
            collective_id=0, has_side_effects=True, vmem_limit_bytes=60416 * 1024
        ),
    )(rows, potential, *consts)
    ev, har = pl.pallas_call(
        result,
        out_shape=(jax.ShapeDtypeStruct(ev.shape, F32), jax.ShapeDtypeStruct(har.shape, F32)),
        in_specs=[pl.BlockSpec(memory_space=pltpu.VMEM)] * 2,
        out_specs=[pl.BlockSpec(memory_space=pl.ANY)] * 2,
        scratch_shapes=[pltpu.SemaphoreType.DMA((9,))],
        compiler_params=pltpu.CompilerParams(vmem_limit_bytes=1024 * 1024),
    )(ev, har)
    return ev.reshape(OWN, XROWS // BANDS, BANDS, 128).transpose(2, 0, 1, 3).reshape(orbitals.shape), har


def solution(mesh):
    return jax.shard_map(
        body,
        mesh=mesh,
        in_specs=(P("band", "slab", None), P("slab", None)),
        out_specs=(P("band", "slab", None), P("slab", None)),
        check_vma=False,
    )
```

```python
import functools
import math

import jax
import jax.numpy as jnp
import ml_dtypes
import numpy as np
from jax import lax
from jax.experimental import pallas as pl
from jax.experimental.pallas import tpu as pltpu
from jax.sharding import PartitionSpec as P

GRID = 96
TIME_STEP = 0.1
MESH = pl.DeviceIdType.MESH
SLABS = 8
GROUPS = 16
BANDS = 4
OWN = GRID // SLABS
LINE = OWN * GRID
TILES = LINE // 128
BLOCK = TILES * 2 * OWN
BAND = SLABS * BLOCK
MODES = 56
PIECES = ((0, 24), (24, 16), (40, 16))
XROWS = 2 * GRID * GRID // 128 * BANDS
PAIRS = GRID // 2
SHARE = GRID // GROUPS
SCALE, TURN = 1.2310180561521498, 4.856431605497022
OFFSET = math.remainder(6 * TURN, 2 * math.pi)
F32 = jnp.float32
BF16 = jnp.bfloat16


def half_step_line():
    n = np.arange(GRID)
    m = (n + GRID // 2) % GRID - GRID // 2
    k = 2.0 * math.pi / GRID * m
    phase = np.exp(1j * (TURN - k * k * TIME_STEP / 4))
    exact = np.fft.ifft(phase) / SCALE
    line = np.stack([exact.real, exact.imag]).astype(np.float32).astype(ml_dtypes.bfloat16).astype(np.float64)

    def worst(values):
        return np.abs(np.fft.fft((values[0] + 1j * values[1]) * SCALE) - phase).max()

    now = worst(line)
    for _ in range(3):
        for part in range(2):
            for t in range(GRID // 2 + 1):
                for sign in (1.0, -1.0):
                    trial = line.copy()
                    step = 2.0 ** (math.floor(math.log2(abs(line[part, t]))) - 7)
                    trial[part, [t, -t % GRID]] = line[part, t] + sign * step
                    error = worst(trial)
                    if error < 0.9999 * now:
                        now, line = error, trial
    return line


def half_step_factor():
    n = np.arange(GRID)
    real, imag = half_step_line()[:, (n[:, None] - n[None, :]) % GRID]
    out = np.zeros((2, GRID, 2, GRID))
    out[0, :, 0] = real
    out[0, :, 1] = -imag
    out[1, :, 0] = imag
    out[1, :, 1] = real
    return out


def real_basis():
    n = np.arange(GRID)
    rows, ksq = [np.full(GRID, 1.0 / math.sqrt(GRID))], [0.0]
    for m in range(1, GRID // 2):
        angle = 2.0 * math.pi * ((m * n) % GRID) / GRID
        rows += [np.cos(angle) * math.sqrt(2.0 / GRID), np.sin(angle) * math.sqrt(2.0 / GRID)]
        ksq += [(2.0 * math.pi * m / GRID) ** 2] * 2
    rows.append(np.where(n % 2 == 0, 1.0, -1.0) / math.sqrt(GRID))
    ksq.append(math.pi**2)
    return np.stack(rows), np.array(ksq)


def exact(matrix):
    return matrix.astype(ml_dtypes.bfloat16)


def split(matrix):
    high = matrix.astype(np.float32).astype(ml_dtypes.bfloat16)
    low = (matrix - high.astype(np.float64)).astype(ml_dtypes.bfloat16)
    return np.stack([high, low])


@functools.lru_cache(maxsize=None)
def tables():
    g = half_step_factor()
    t = {}
    into = g.transpose(2, 3, 0, 1)
    padded = np.zeros((2, GRID, 2, 128))
    padded[..., :GRID] = into
    padded = padded.reshape(2 * GRID, 256)
    za = np.zeros((2, 256, 256))
    za[0, :192] = padded
    za[1, 64:] = padded
    t["z_in"] = exact(za.reshape(512, 256))
    rows = np.zeros((2, 128, 2, GRID))
    rows[:, :GRID] = into
    rows = rows.reshape(256, 2 * GRID)
    zb = np.zeros((2, 256, 256))
    zb[0, :, :192] = rows
    zb[1, :, 64:] = rows
    t["z_out"] = exact(zb.reshape(512, 256))
    j, s, a = np.meshgrid(np.arange(4), np.arange(SLABS), np.arange(3), indexing="ij")
    wire_y = 12 * s + 4 * a + j
    pair_y = 2 * np.arange(PAIRS)[None, :] + np.arange(2)[:, None]
    ky = g[:, wire_y][:, :, :, :, :, pair_y]
    t["y_in"] = exact(ky.transpose(1, 0, 2, 3, 5, 4, 6).reshape(192, 192))
    ky = g[:, pair_y][:, :, :, :, wire_y]
    t["y_out"] = exact(ky.transpose(1, 0, 2, 4, 3, 5, 6).reshape(192, 192))
    kx = g.reshape(2, GRID, 2, SLABS, 3, 4)
    t["x_in"] = exact(kx.transpose(0, 1, 3, 4, 2, 5).reshape(192, 192))
    kx = g.reshape(2, SLABS, 3, 4, 2, GRID)
    t["x_out"] = exact(kx.transpose(1, 2, 0, 3, 4, 5).reshape(192, 192))
    q, ksq = real_basis()
    qx = np.zeros((GROUPS, 8, GRID))
    qx[:, :SHARE] = q.reshape(GROUPS, SHARE, GRID)
    qx = qx.reshape(128, GRID)
    t["qx"] = split(qx * SCALE**6).reshape(256, GRID)
    t["qxt"] = split(qx.T).reshape(192, 128)
    qz = np.zeros((128, 128))
    qz[:GRID, :GRID] = q.T
    t["qz"] = split(qz).reshape(256, 128)
    t["qzt"] = split(qz.T).reshape(256, 128)
    aj_s = 12 * np.arange(SLABS)[None, :] + np.arange(OWN)[:, None]
    t["qy"] = split(q[:, aj_s.reshape(-1)]).reshape(192, GRID)
    qyt = np.zeros((SLABS, 16, GRID))
    qyt[:, :OWN] = q.T.reshape(SLABS, OWN, GRID)
    t["qyt"] = split(qyt).transpose(1, 0, 2, 3).reshape(SLABS, 32, GRID)
    kxz = np.ones((GROUPS, 8, 128))
    kxz[:, :SHARE, :GRID] = ksq.reshape(GROUPS, SHARE)[:, :, None] + ksq[None, None, :]
    t["kxz"] = kxz.astype(np.float32)
    t["ky2"] = np.broadcast_to(ksq[:, None], (GRID, 128)).astype(np.float32)
    return t


NAMES = ("z_in", "y_in", "x_in", "kxz", "ky2", "qx", "qz", "qy", "qyt", "qzt", "qxt", "x_out", "y_out", "z_out")


def halves(x):
    high = x.astype(BF16)
    return high, (x - high.astype(F32)).astype(BF16)


def dot(a, b):
    return jnp.dot(a, b, preferred_element_type=F32)


def times(x, high, low):
    xh, xl = halves(x)
    return dot(xh, high) + (dot(xl, high) + dot(xh, low))


def left(high, low, x):
    xh, xl = halves(x)
    return dot(high, xh) + (dot(high, xl) + dot(low, xh))


def sin_cos(t):
    n = jnp.round(t * (2.0 / math.pi))
    r = t - n * 1.5703125
    r = r - n * 4.8375129699707031e-4
    r = r - n * 7.5495649e-08
    r2 = r * r
    sine = r + r * r2 * (-1.6666654611e-1 + r2 * (8.3321608736e-3 + r2 * -1.9515295891e-4))
    cosine = 1.0 - 0.5 * r2 + r2 * r2 * (4.166664568298827e-2 + r2 * (-1.388731625493765e-3 + r2 * 2.443315711809948e-5))
    quarter = n.astype(jnp.int32) & 3
    odd = (quarter & 1) == 1
    s = jnp.where(odd, cosine, sine)
    c = jnp.where(odd, sine, cosine)
    s = jnp.where(quarter >= 2, -s, s)
    c = jnp.where((quarter == 1) | (quarter == 2), -c, c)
    return s, c


def times2(x, table):
    r = dot(jnp.concatenate(halves(x), 0), table)
    return r[: x.shape[0]] + r[x.shape[0] :]


def left2(table, x):
    r = dot(table, jnp.concatenate(halves(x), 1))
    return r[:, : x.shape[1]] + r[:, x.shape[1] :]


def lane_of(shape):
    return lax.broadcasted_iota(jnp.int32, shape, len(shape) - 1)


def packed(parts):
    lane = lane_of(parts[0].shape)
    r1 = pltpu.roll(parts[1], 96, 1)
    r2 = pltpu.roll(parts[2], 64, 1)
    r3 = pltpu.roll(parts[3], 32, 1)
    return (
        jnp.where(lane < 96, parts[0], r1),
        jnp.where(lane < 64, r1, r2),
        jnp.where(lane < 32, r2, r3),
    )


def unpacked(tiles):
    lane = lane_of(tiles[0].shape)
    return (
        tiles[0],
        pltpu.roll(jnp.where(lane < 64, tiles[1], tiles[0]), 32, 1),
        pltpu.roll(jnp.where(lane < 32, tiles[2], tiles[1]), 64, 1),
        pltpu.roll(tiles[2], 96, 1),
    )


def kernel(orb, pot, *refs):
    sources, refs = refs[: len(NAMES)], refs[len(NAMES) :]
    ev, har, refs = refs[0], refs[1], refs[2:]
    consts, refs = refs[: len(NAMES)], refs[len(NAMES) :]
    z_in, y_in, x_in, kxz, ky2, qx, qz, qy, qyt, qzt, qxt, x_out, y_out, z_out = consts
    (
     ib, wire, lines, moved, back, home, dens, dq, part, share, modes, whole, zt, green, hq, hart,
           vb, vl, cosb, sinb, hs, hrow,
           in_sem, pot_s, pot_r, w_s, w_r, b_s, b_r, rs_s, rs_r, ag_s, ag_r, hq_s, hq_r, h_s, h_r, g_s, g_r, own_sem, const_sem, tail_r, head_r, first_r, last_r) = refs
    me = lax.axis_index("slab")
    grp = lax.axis_index("band")
    slab_peers = [
        (2 * i + j, lax.rem(me // 2 + i, 4) * 2 + lax.rem(me + j, 2))
        for i, j in ((2, 0), (2, 1), (1, 0), (3, 0), (1, 1), (3, 1), (0, 1))
    ]
    offsets = sorted(
        [(i, j) for i in range(4) for j in range(4) if i or j],
        key=lambda o: -min(o[0], 4 - o[0]) - min(o[1], 4 - o[1]),
    )
    band_peers = [
        (4 * i + j, lax.rem(grp // 4 + i, 4) * 4 + lax.rem(lax.rem(grp, 4) + j, 4)) for i, j in offsets
    ]

    barrier = pltpu.get_barrier_semaphore()
    for _, q in slab_peers:
        pl.semaphore_signal(barrier, inc=1, device_id={"slab": q}, device_id_type=MESH)
    for _, q in band_peers:
        pl.semaphore_signal(barrier, inc=1, device_id={"band": q}, device_id_type=MESH)

    def load(i):
        at = pl.ds(i * 2 * XROWS, 2 * XROWS)
        return pltpu.make_async_copy(orb.at[at], ib.at[at], in_sem.at[i])

    def table(i):
        return pltpu.make_async_copy(sources[i], consts[i], const_sem.at[i])

    table(0).start()
    table(1).start()
    for i in range(OWN // 2):
        load(i).start()
    for i in range(2, len(NAMES)):
        table(i).start()
    table(0).wait()
    table(1).wait()

    def slab_copy(src, dst, s, r, q):
        return pltpu.make_async_remote_copy(src, dst, s, r, device_id={"slab": q}, device_id_type=MESH)

    def band_copy(src, dst, s, r, q):
        return pltpu.make_async_remote_copy(src, dst, s, r, device_id={"band": q}, device_id_type=MESH)

    def row_of(pair):
        return pair // 2 * 8 + lax.rem(pair, 2) * 2

    def quad(ref, b, q, k):
        return ref.reshape(BANDS * SLABS * TILES, 24, 128).at[pl.ds((b * SLABS + q) * TILES, TILES), pl.ds(pl.multiple_of(8 * k, 8), 8)]

    def quad_copy(src, dst, b, k, d, q, send, recv):
        return slab_copy(quad(src, b, q, k), quad(dst, b, me, k), send.at[0], recv.at[k], q)

    def send_first(k, d, q):
        return quad_copy(wire, lines, 0, k, d, q, w_s, first_r)

    def send_last(k, d, q):
        return quad_copy(back, home, BANDS - 1, k, d, q, b_s, last_r)

    def done(view, sem):
        pltpu.make_async_copy(view, view, sem).wait()

    def rows(ref, n):
        return ref.at[pl.ds(0, n)]

    OTHERS, REST = SLABS - 1, GROUPS - 1

    def first(b, carry):
        def local(pair, carry):
            @pl.when(b == 0)
            def _():
                load(pair).wait()

            tiles = [
                jnp.concatenate(
                    [ib[pl.ds((2 * pair + i) * XROWS + 4 * t + b, PAIRS, stride=12), :] for i in range(2)], 0
                )
                for t in range(3)
            ]
            z = []
            for j in range(2):
                x = jnp.concatenate([tiles[j], tiles[j + 1]], 1)
                z.append(times2(x, z_in[pl.ds(256 * j, 256)]))
            x = jnp.concatenate(
                [
                    jnp.concatenate(
                        [z[j][48 * i : 48 * i + 48, 128 * c : 128 * c + 128] for j in range(2) for c in range(2)], 0
                    )
                    for i in range(2)
                ],
                1,
            )
            r = left2(y_in[...], x)
            for i in range(2):
                x = 2 * pair + i
                tiles = packed([r[48 * j : 48 * j + 48, 128 * i : 128 * i + 128] for j in range(4)])
                for t in range(3):
                    for c in range(2):
                        wire[pl.ds(b * BAND + t * 24 + 4 * c + row_of(pair) + i, 24, stride=72), :] = tiles[t][24 * c : 24 * c + 24]

            @pl.when((b == 0) & (pair == 1))
            def _():
                pl.semaphore_wait(barrier, SLABS - 1 + GROUPS - 1)

            @pl.when((b == 0) & (lax.rem(pair, 2) == 1))
            def _():
                for d, q in slab_peers:
                    send_first(pair // 2, d, q).start()

            return carry

        lax.fori_loop(0, OWN // 2, local, 0)

        @pl.when((b > 0) & (b < BANDS - 1))
        def _():
            for d, q in slab_peers:
                send_line(b, d, q).start()

        @pl.when(b == BANDS - 1)
        def _():
            for a in range(3):
                for d, q in slab_peers:
                    send_tail(a, d, q).start()

        own_line(b).start()
        return carry

    def send_tail(a, d, q):
        return slab_copy(
            wire.at[pl.ds((BANDS - 1) * BAND + q * BLOCK + 72 * a, 72)],
            lines.at[pl.ds((BANDS - 1) * BAND + me * BLOCK + 72 * a, 72)],
            w_s.at[0],
            tail_r.at[a],
            q,
        )

    def send_line(b, d, q):
        return slab_copy(
            wire.at[pl.ds(b * BAND + q * BLOCK, BLOCK)],
            lines.at[pl.ds(b * BAND + me * BLOCK, BLOCK)],
            w_s.at[0],
            w_r.at[b],
            q,
        )

    def own_line(b):
        at = pl.ds(b * BAND + me * BLOCK, BLOCK)
        return pltpu.make_async_copy(wire.at[at], lines.at[at], own_sem.at[b])

    lax.fori_loop(0, BANDS, first, 0)

    def send_pot(d, q):
        return slab_copy(
            pot.at[:, pl.ds(pl.multiple_of(q * LINE, 128), LINE)], vb.at[me], pot_s.at[0], pot_r.at[0], q
        )

    for d, q in slab_peers:
        send_pot(d, q).start()
    own_pot = pltpu.make_async_copy(
        pot.at[:, pl.ds(pl.multiple_of(me * LINE, 128), LINE)], vb.at[me], own_sem.at[BANDS]
    )
    own_pot.start()

    for i in range(2, len(NAMES)):
        table(i).wait()

    for i in range(8):
        ksq = ky2[...] + kxz[grp, i : i + 1, :]
        zero = ksq == 0.0
        green[:, 128 * i : 128 * i + 128] = jnp.where(zero, 0.0, 4.0 * math.pi / jnp.where(zero, 1.0, ksq))

    dens[...] = jnp.zeros_like(dens)

    def kx_in(b, a):
        x = jnp.concatenate(
            [
                jnp.concatenate(
                    [lines[pl.ds(b * BAND + s * BLOCK + (3 * a + t) * 24, 24)] for s in range(SLABS)], 0
                )
                for t in range(3)
            ],
            1,
        )
        r = left2(x_in[...], x)
        at = pl.ds(pl.multiple_of(a * 384, 128), 384)
        moved[b, :, at] = r
        dens[:, at] += r[:GRID] * r[:GRID] + r[GRID:] * r[GRID:]

    def lines_x(b, carry):
        own_line(b).wait()

        @pl.when(b == 0)
        def _():
            for k in range(3):
                done(rows(lines, OTHERS * 72), first_r.at[k])

        @pl.when(b > 0)
        def _():
            done(rows(lines, OTHERS * BLOCK), w_r.at[b])

        def chunk(a, carry):
            kx_in(b, a)
            return carry

        lax.fori_loop(0, 3, chunk, 0)
        return carry

    lax.fori_loop(0, BANDS - 1, lines_x, 0)

    def send_part(a, d, q):
        at = pl.ds(pl.multiple_of(a * 384, 128), 384)
        return band_copy(dq.at[pl.ds(pl.multiple_of(q * 8, 8), 8), at], part.at[grp, :, at], rs_s.at[0], rs_r.at[a], q)

    own_line(BANDS - 1).wait()

    def last_lines(a, carry):
        done(rows(lines, OTHERS * 72), tail_r.at[a])
        kx_in(BANDS - 1, a)
        at = pl.ds(pl.multiple_of(a * 384, 128), 384)
        dq[:, at] = left(qx[pl.ds(0, 128)], qx[pl.ds(128, 128)], dens[:, at])
        for d, q in band_peers:
            send_part(a, d, q).start()
        return carry

    lax.fori_loop(0, 3, last_lines, 0)

    own_pot.wait()
    done(rows(vb, OTHERS), pot_r.at[0])
    for s in range(SLABS):
        vl[OWN * s : OWN * s + OWN, :] = vb[s]

    def send_share(a, d, q):
        at = pl.ds(pl.multiple_of(a * 384, 128), 384)
        return slab_copy(share.at[:, at], whole.at[me, :, at], ag_s.at[0], ag_r.at[a], q)

    def sums(a, carry):
        at = pl.ds(pl.multiple_of(a * 384, 128), 384)
        done(part.at[pl.ds(0, REST), :, at], rs_r.at[a])
        total = dq[pl.ds(pl.multiple_of(grp * 8, 8), 8), at]
        for d, q in band_peers:
            total = total + part[q, :, at]
        share[:, at] = total
        for d, q in slab_peers:
            send_share(a, d, q).start()
        whole[me, :, at] = total
        return carry

    lax.fori_loop(0, 3, sums, 0)

    def along_z(a, carry):
        done(whole.at[pl.ds(0, OTHERS), :, pl.ds(pl.multiple_of(a * 384, 128), 384)], ag_r.at[a])
        tiles = [
            jnp.concatenate(
                [whole[s, :, pl.ds(pl.multiple_of(384 * a + 128 * t, 128), 128)] for s in range(SLABS)], 0
            )
            for t in range(3)
        ]
        x = jnp.concatenate(unpacked(tiles), 0)
        zt[pl.ds(pl.multiple_of(256 * a, 256), 256)] = times(x, qz[pl.ds(0, 128)], qz[pl.ds(128, 128)])
        return carry

    lax.fori_loop(0, 3, along_z, 0)
    x = jnp.concatenate([zt[pl.ds(i, GRID, stride=8), :] for i in range(8)], 1)
    x = left(qy[pl.ds(0, GRID)], qy[pl.ds(GRID, GRID)], x) * green[...]
    x = left(qyt[me, 0:16], qyt[me, 16:32], x)
    x = jnp.concatenate([x[:, 128 * i : 128 * i + 128] for i in range(8)], 0)
    zt[pl.ds(0, 128)] = times(x, qzt[pl.ds(0, 128)], qzt[pl.ds(128, 128)])
    for a in range(3):
        tiles = packed([zt[pl.ds(4 * a + j, 8, stride=16), :] for j in range(4)])
        for t in range(3):
            modes[SHARE * (3 * a + t) : SHARE * (3 * a + t) + 8, :] = tiles[t]

    def send_modes(k, d, q):
        start, rows = PIECES[k]
        return band_copy(
            modes.at[pl.ds(start, rows)],
            hq.at[pl.ds(grp * MODES + start, rows)],
            hq_s.at[0],
            hq_r.at[k],
            q,
        )

    for k in range(3):
        for d, q in band_peers:
            send_modes(k, d, q).start()
    hq[pl.ds(pl.multiple_of(grp * MODES, 8), MODES)] = modes[...]

    def send_back(b, d, q):
        return slab_copy(
            back.at[pl.ds(b * BAND + q * BLOCK, BLOCK)],
            home.at[pl.ds(b * BAND + me * BLOCK, BLOCK)],
            b_s.at[0],
            b_r.at[b],
            q,
        )

    def own_back(b):
        at = pl.ds(b * BAND + me * BLOCK, BLOCK)
        return pltpu.make_async_copy(back.at[at], home.at[at], own_sem.at[b])

    def send_head(a, d, q):
        return slab_copy(
            back.at[pl.ds(q * BLOCK + 72 * a, 72)],
            home.at[pl.ds(me * BLOCK + 72 * a, 72)],
            b_s.at[0],
            head_r.at[a],
            q,
        )

    def kx_out(b, a):
        at = pl.ds(pl.multiple_of(a * 384, 128), 384)
        re = moved[b, 0:GRID, at]
        im = moved[b, GRID : 2 * GRID, at]
        cs = cosb[:, at]
        sn = sinb[:, at]
        x = jnp.concatenate([re * cs + im * sn, im * cs - re * sn], 0)
        r = left2(x_out[...], x)
        for q in range(SLABS):
            for t in range(3):
                back[pl.ds(b * BAND + q * BLOCK + (3 * a + t) * 24, 24)] = r[24 * q : 24 * q + 24, 128 * t : 128 * t + 128]

    for a in range(3):
        done(rows(hq, REST * PIECES[a][1]), hq_r.at[a])
        at = pl.ds(384 * a, 384)
        x = jnp.concatenate(
            [
                jnp.concatenate(
                    [
                        hq[MODES * g + SHARE * (3 * a + t) : MODES * g + SHARE * (3 * a + t) + 8, :]
                        for g in range(GROUPS)
                    ],
                    0,
                )
                for t in range(3)
            ],
            1,
        )
        h = left(qxt[pl.ds(0, GRID)], qxt[pl.ds(GRID, GRID)], x)
        hart[:, at] = h
        s, c = sin_cos((vl[:, at] + h) * TIME_STEP + OFFSET)
        sinb[:, at] = s * SCALE**6
        cosb[:, at] = c * SCALE**6
        kx_out(0, a)
        for d, q in slab_peers:
            send_head(a, d, q).start()
    own_back(0).start()

    for t in range(TILES):
        hs[pl.ds(t, GRID, stride=16), :] = hart[:, 128 * t : 128 * t + 128]

    def send_row(d, q):
        return slab_copy(
            hs.at[pl.ds((q * OWN + grp) * 16, 16)],
            hrow.at[pl.ds((grp * SLABS + me) * 16, 16)],
            h_s.at[0],
            h_r.at[0],
            q,
        )

    own_row = pltpu.make_async_copy(
        hs.at[pl.ds((me * OWN + grp) * 16, 16)], hrow.at[pl.ds((grp * SLABS + me) * 16, 16)], own_sem.at[BANDS]
    )

    def send_rows(d, q, g):
        at = pl.ds(g * (SLABS * 16), SLABS * 16)
        return band_copy(hrow.at[at], hrow.at[at], g_s.at[0], g_r.at[0], q)

    @pl.when(grp < OWN)
    def _():
        own_row.start()
        for d, q in slab_peers:
            send_row(d, q).start()

    def kick(b, carry):
        def chunk(a, carry):
            kx_out(b, a)
            return carry

        lax.fori_loop(0, 3, chunk, 0)
        @pl.when(b < BANDS - 1)
        def _():
            for d, q in slab_peers:
                send_back(b, d, q).start()

        @pl.when(b == BANDS - 1)
        def _():
            for k in range(3):
                for d, q in slab_peers:
                    send_last(k, d, q).start()

        own_back(b).start()
        return carry

    lax.fori_loop(1, BANDS, kick, 0)

    def rows_out():
        @pl.when(grp < OWN)
        def _():
            own_row.wait()
            done(rows(hrow, OTHERS * 16), h_r.at[0])
            for d, q in band_peers:
                send_rows(d, q, grp).start()

    def rows_in():
        @pl.when(grp < OWN)
        def _():
            done(rows(hrow, (OWN - 1) * SLABS * 16), g_r.at[0])

        @pl.when(grp >= OWN)
        def _():
            done(rows(hrow, OWN * SLABS * 16), g_r.at[0])

        for s in range(SLABS):
            for t in range(TILES):
                har[:, LINE * s + 128 * t : LINE * s + 128 * t + 128] = hrow[
                    pl.ds(16 * s + t, OWN, stride=SLABS * 16), :
                ]

    def last(b, carry):
        @pl.when(b == 1)
        def _():
            rows_out()

        @pl.when(b == 3)
        def _():
            rows_in()

        own_back(b).wait()

        @pl.when(b == 0)
        def _():
            for a in range(3):
                done(rows(home, OTHERS * 72), head_r.at[a])

        @pl.when((b > 0) & (b < BANDS - 1))
        def _():
            done(rows(home, OTHERS * BLOCK), b_r.at[b])

        def local(pair, carry):
            @pl.when((b == BANDS - 1) & (lax.rem(pair, 2) == 0))
            def _():
                done(rows(home, OTHERS * 72), last_r.at[pair // 2])

            cols = []
            for i in range(2):
                x = 2 * pair + i
                tiles = [
                    jnp.concatenate(
                        [home[pl.ds(b * BAND + t * 24 + 4 * c + row_of(pair) + i, 24, stride=72), :] for c in range(2)], 0
                    )
                    for t in range(3)
                ]
                cols.append(jnp.concatenate(unpacked(tiles), 0))
            r = left2(y_out[...], jnp.concatenate(cols, 1))
            res = []
            for j in range(2):
                x = jnp.concatenate(
                    [
                        jnp.concatenate(
                            [r[96 * j + 48 * c : 96 * j + 48 * c + 48, 128 * i : 128 * i + 128] for c in range(2)], 1
                        )
                        for i in range(2)
                    ],
                    0,
                )
                res.append(times2(x, z_out[pl.ds(256 * j, 256)]))
            tiles = (res[0][:, :128], res[0][:, 128:] + res[1][:, :128], res[1][:, 128:])
            for i in range(2):
                for t in range(3):
                    ev[pl.ds((2 * pair + i) * XROWS + 4 * t + b, PAIRS, stride=12), :] = tiles[t][48 * i : 48 * i + 48]

            return carry

        lax.fori_loop(0, OWN // 2, local, 0)
        return carry

    lax.fori_loop(0, BANDS, last, 0)

    @pl.when(grp < OWN)
    def _():
        done(rows(hs, OTHERS * 16), h_s.at[0])
        done(rows(wire, REST * SLABS * 16), g_s.at[0])

    done(rows(vb, OTHERS), pot_s.at[0])
    done(rows(wire, 3 * OTHERS * 24), ag_s.at[0])
    done(rows(wire, 3 * REST * 24), rs_s.at[0])
    done(rows(wire, REST * MODES), hq_s.at[0])
    done(rows(wire, BANDS * OTHERS * BLOCK), w_s.at[0])
    done(rows(back, BANDS * OTHERS * BLOCK), b_s.at[0])


def result(ev, har, ev_out, har_out, sem):
    n = ev.shape[0] // 8
    copies = [
        pltpu.make_async_copy(ev.at[pl.ds(n * i, n)], ev_out.at[pl.ds(n * i, n)], sem.at[i]) for i in range(8)
    ]
    copies.append(pltpu.make_async_copy(har, har_out, sem.at[8]))
    for copy in copies:
        copy.start()
    for copy in copies:
        copy.wait()


def body(orbitals, potential):
    rows = orbitals.reshape(BANDS, OWN, XROWS // BANDS, 128).transpose(1, 2, 0, 3).reshape(OWN * XROWS, 128)
    t = tables()
    consts = [jnp.asarray(t[name]) for name in NAMES]
    vmem = lambda *shape: pltpu.VMEM(shape, F32)
    dma = lambda *shape: pltpu.SemaphoreType.DMA(shape)
    ev, har = pl.pallas_call(
        kernel,
        out_shape=(
            pltpu.VMEM((OWN * XROWS, 128), F32),
            pltpu.VMEM(potential.shape, F32),
        ),
        in_specs=[pl.BlockSpec(memory_space=pl.ANY)] * (2 + len(consts)),
        out_specs=[pl.BlockSpec(memory_space=pltpu.VMEM)] * 2,
        scratch_shapes=[pltpu.VMEM(c.shape, c.dtype) for c in consts]
        + [
            vmem(OWN * XROWS, 128),
            vmem(BANDS * BAND, 128),
            vmem(BANDS * BAND, 128),
            vmem(BANDS, 2 * GRID, LINE),
            vmem(BANDS * BAND, 128),
            vmem(BANDS * BAND, 128),
            vmem(GRID, LINE),
            vmem(128, LINE),
            vmem(GROUPS, 8, LINE),
            vmem(8, LINE),
            vmem(MODES, 128),
            vmem(SLABS, 8, LINE),
            vmem(768, 128),
            vmem(GRID, 1024),
            vmem(GROUPS * MODES, 128),
            vmem(GRID, LINE),
            vmem(SLABS, OWN, LINE),
            vmem(GRID, LINE),
            vmem(GRID, LINE),
            vmem(GRID, LINE),
            vmem(GRID * 16, 128),
            vmem(OWN * SLABS * 16, 128),
            dma(OWN // 2),
            dma(1), dma(1),
            dma(1), dma(BANDS),
            dma(1), dma(BANDS),
            dma(1), dma(3),
            dma(1), dma(3),
            dma(1), dma(3),
            dma(1), dma(1),
            dma(1), dma(1),
            dma(BANDS + 1),
            dma(len(consts)),
            dma(3), dma(3), dma(3), dma(3),
        ],
        compiler_params=pltpu.CompilerParams(
            collective_id=0, has_side_effects=True, vmem_limit_bytes=60416 * 1024
        ),
    )(rows, potential, *consts)
    ev, har = pl.pallas_call(
        result,
        out_shape=(jax.ShapeDtypeStruct(ev.shape, F32), jax.ShapeDtypeStruct(har.shape, F32)),
        in_specs=[pl.BlockSpec(memory_space=pltpu.VMEM)] * 2,
        out_specs=[pl.BlockSpec(memory_space=pl.ANY)] * 2,
        scratch_shapes=[pltpu.SemaphoreType.DMA((9,))],
        compiler_params=pltpu.CompilerParams(vmem_limit_bytes=1024 * 1024),
    )(ev, har)
    return ev.reshape(OWN, XROWS // BANDS, BANDS, 128).transpose(2, 0, 1, 3).reshape(orbitals.shape), har


def solution(mesh):
    return jax.shard_map(
        body,
        mesh=mesh,
        in_specs=(P("band", "slab", None), P("slab", None)),
        out_specs=(P("band", "slab", None), P("slab", None)),
        check_vma=False,
    )
```

```python
import functools
import math

import jax
import jax.numpy as jnp
import ml_dtypes
import numpy as np
from jax import lax
from jax.experimental import pallas as pl
from jax.experimental.pallas import tpu as pltpu
from jax.sharding import PartitionSpec as P

GRID = 96
TIME_STEP = 0.1
MESH = pl.DeviceIdType.MESH
SLABS = 8
GROUPS = 16
BANDS = 4
OWN = GRID // SLABS
LINE = OWN * GRID
TILES = LINE // 128
BLOCK = TILES * 2 * OWN
BAND = SLABS * BLOCK
CHUNKS = ((0, 4), (4, 3), (7, 2))
MODES = 56
PIECES = ((0, 16), (16, 16), (32, 24))
HEADS = ((0, 2), (2, 3), (5, 4))
XROWS = 2 * GRID * GRID // 128 * BANDS
PAIRS = GRID // 2
SHARE = GRID // GROUPS
SCALE, TURN = 1.2310180561521498, 4.856431605497022
OFFSET = math.remainder(6 * TURN, 2 * math.pi)
F32 = jnp.float32
BF16 = jnp.bfloat16


def half_step_line():
    n = np.arange(GRID)
    m = (n + GRID // 2) % GRID - GRID // 2
    k = 2.0 * math.pi / GRID * m
    phase = np.exp(1j * (TURN - k * k * TIME_STEP / 4))
    exact = np.fft.ifft(phase) / SCALE
    line = np.stack([exact.real, exact.imag]).astype(np.float32).astype(ml_dtypes.bfloat16).astype(np.float64)

    def worst(values):
        return np.abs(np.fft.fft((values[0] + 1j * values[1]) * SCALE) - phase).max()

    now = worst(line)
    for _ in range(3):
        for part in range(2):
            for t in range(GRID // 2 + 1):
                for sign in (1.0, -1.0):
                    trial = line.copy()
                    step = 2.0 ** (math.floor(math.log2(abs(line[part, t]))) - 7)
                    trial[part, [t, -t % GRID]] = line[part, t] + sign * step
                    error = worst(trial)
                    if error < 0.9999 * now:
                        now, line = error, trial
    return line


def half_step_factor():
    n = np.arange(GRID)
    real, imag = half_step_line()[:, (n[:, None] - n[None, :]) % GRID]
    out = np.zeros((2, GRID, 2, GRID))
    out[0, :, 0] = real
    out[0, :, 1] = -imag
    out[1, :, 0] = imag
    out[1, :, 1] = real
    return out


def real_basis():
    n = np.arange(GRID)
    rows, ksq = [np.full(GRID, 1.0 / math.sqrt(GRID))], [0.0]
    for m in range(1, GRID // 2):
        angle = 2.0 * math.pi * ((m * n) % GRID) / GRID
        rows += [np.cos(angle) * math.sqrt(2.0 / GRID), np.sin(angle) * math.sqrt(2.0 / GRID)]
        ksq += [(2.0 * math.pi * m / GRID) ** 2] * 2
    rows.append(np.where(n % 2 == 0, 1.0, -1.0) / math.sqrt(GRID))
    ksq.append(math.pi**2)
    return np.stack(rows), np.array(ksq)


def exact(matrix):
    return matrix.astype(ml_dtypes.bfloat16)


def split(matrix):
    high = matrix.astype(np.float32).astype(ml_dtypes.bfloat16)
    low = (matrix - high.astype(np.float64)).astype(ml_dtypes.bfloat16)
    return np.stack([high, low])


@functools.lru_cache(maxsize=None)
def tables():
    g = half_step_factor()
    t = {}
    into = g.transpose(2, 3, 0, 1)
    padded = np.zeros((2, GRID, 2, 128))
    padded[..., :GRID] = into
    padded = padded.reshape(2 * GRID, 256)
    za = np.zeros((2, 256, 256))
    za[0, :192] = padded
    za[1, 64:] = padded
    t["z_in"] = exact(za.reshape(512, 256))
    rows = np.zeros((2, 128, 2, GRID))
    rows[:, :GRID] = into
    rows = rows.reshape(256, 2 * GRID)
    zb = np.zeros((2, 256, 256))
    zb[0, :, :192] = rows
    zb[1, :, 64:] = rows
    t["z_out"] = exact(zb.reshape(512, 256))
    j, s, a = np.meshgrid(np.arange(4), np.arange(SLABS), np.arange(3), indexing="ij")
    wire_y = 12 * s + 4 * a + j
    pair_y = 2 * np.arange(PAIRS)[None, :] + np.arange(2)[:, None]
    ky = g[:, wire_y][:, :, :, :, :, pair_y]
    t["y_in"] = exact(ky.transpose(1, 0, 2, 3, 5, 4, 6).reshape(192, 192))
    ky = g[:, pair_y][:, :, :, :, wire_y]
    t["y_out"] = exact(ky.transpose(1, 0, 2, 4, 3, 5, 6).reshape(192, 192))
    kx = g.reshape(2, GRID, 2, SLABS, 3, 4)
    t["x_in"] = exact(kx.transpose(0, 1, 3, 4, 2, 5).reshape(192, 192))
    kx = g.reshape(2, SLABS, 3, 4, 2, GRID)
    t["x_out"] = exact(kx.transpose(1, 2, 0, 3, 4, 5).reshape(192, 192))
    q, ksq = real_basis()
    qx = np.zeros((GROUPS, 8, GRID))
    qx[:, :SHARE] = q.reshape(GROUPS, SHARE, GRID)
    qx = qx.reshape(128, GRID)
    t["qx"] = split(qx * SCALE**6).reshape(256, GRID)
    t["qxt"] = split(qx.T).reshape(192, 128)
    qz = np.zeros((128, 128))
    qz[:GRID, :GRID] = q.T
    t["qz"] = split(qz).reshape(256, 128)
    t["qzt"] = split(qz.T).reshape(256, 128)
    aj_s = 12 * np.arange(SLABS)[None, :] + np.arange(OWN)[:, None]
    t["qy"] = split(q[:, aj_s.reshape(-1)]).reshape(192, GRID)
    qyt = np.zeros((SLABS, 16, GRID))
    qyt[:, :OWN] = q.T.reshape(SLABS, OWN, GRID)
    t["qyt"] = split(qyt).transpose(1, 0, 2, 3).reshape(SLABS, 32, GRID)
    kxz = np.ones((GROUPS, 8, 128))
    kxz[:, :SHARE, :GRID] = ksq.reshape(GROUPS, SHARE)[:, :, None] + ksq[None, None, :]
    t["kxz"] = kxz.astype(np.float32)
    t["ky2"] = np.broadcast_to(ksq[:, None], (GRID, 128)).astype(np.float32)
    return t


NAMES = ("z_in", "y_in", "x_in", "kxz", "ky2", "qx", "qz", "qy", "qyt", "qzt", "qxt", "x_out", "y_out", "z_out")


def halves(x):
    high = x.astype(BF16)
    return high, (x - high.astype(F32)).astype(BF16)


def dot(a, b):
    return jnp.dot(a, b, preferred_element_type=F32)


def times(x, high, low):
    xh, xl = halves(x)
    return dot(xh, high) + (dot(xl, high) + dot(xh, low))


def left(high, low, x):
    xh, xl = halves(x)
    return dot(high, xh) + (dot(high, xl) + dot(low, xh))


def sin_cos(t):
    n = jnp.round(t * (2.0 / math.pi))
    r = t - n * 1.5703125
    r = r - n * 4.8375129699707031e-4
    r = r - n * 7.5495649e-08
    r2 = r * r
    sine = r + r * r2 * (-1.6666654611e-1 + r2 * (8.3321608736e-3 + r2 * -1.9515295891e-4))
    cosine = 1.0 - 0.5 * r2 + r2 * r2 * (4.166664568298827e-2 + r2 * (-1.388731625493765e-3 + r2 * 2.443315711809948e-5))
    quarter = n.astype(jnp.int32) & 3
    odd = (quarter & 1) == 1
    s = jnp.where(odd, cosine, sine)
    c = jnp.where(odd, sine, cosine)
    s = jnp.where(quarter >= 2, -s, s)
    c = jnp.where((quarter == 1) | (quarter == 2), -c, c)
    return s, c


def times2(x, table):
    r = dot(jnp.concatenate(halves(x), 0), table)
    return r[: x.shape[0]] + r[x.shape[0] :]


def left2(table, x):
    r = dot(table, jnp.concatenate(halves(x), 1))
    return r[:, : x.shape[1]] + r[:, x.shape[1] :]


def lane_of(shape):
    return lax.broadcasted_iota(jnp.int32, shape, len(shape) - 1)


def packed(parts):
    lane = lane_of(parts[0].shape)
    r1 = pltpu.roll(parts[1], 96, 1)
    r2 = pltpu.roll(parts[2], 64, 1)
    r3 = pltpu.roll(parts[3], 32, 1)
    return (
        jnp.where(lane < 96, parts[0], r1),
        jnp.where(lane < 64, r1, r2),
        jnp.where(lane < 32, r2, r3),
    )


def unpacked(tiles):
    lane = lane_of(tiles[0].shape)
    return (
        tiles[0],
        pltpu.roll(jnp.where(lane < 64, tiles[1], tiles[0]), 32, 1),
        pltpu.roll(jnp.where(lane < 32, tiles[2], tiles[1]), 64, 1),
        pltpu.roll(tiles[2], 96, 1),
    )


def kernel(orb, pot, *refs):
    sources, refs = refs[: len(NAMES)], refs[len(NAMES) :]
    ev, har, refs = refs[0], refs[1], refs[2:]
    consts, refs = refs[: len(NAMES)], refs[len(NAMES) :]
    z_in, y_in, x_in, kxz, ky2, qx, qz, qy, qyt, qzt, qxt, x_out, y_out, z_out = consts
    (
     ib, wire, lines, moved, back, home, dens, dq, part, share, modes, whole, zt, green, hq, hart,
           vb, vl, cosb, sinb, hs, hrow,
           in_sem, pot_s, pot_r, w_s, w_r, b_s, b_r, rs_s, rs_r, ag_s, ag_r, hq_s, hq_r, h_s, h_r, g_s, g_r, own_sem, const_sem, tail_r, head_r, first_r, last_r) = refs
    me = lax.axis_index("slab")
    grp = lax.axis_index("band")
    slab_peers = [
        (2 * i + j, lax.rem(me // 2 + i, 4) * 2 + lax.rem(me + j, 2))
        for i, j in ((2, 0), (2, 1), (1, 0), (3, 0), (1, 1), (3, 1), (0, 1))
    ]
    offsets = sorted(
        [(i, j) for i in range(4) for j in range(4) if i or j],
        key=lambda o: -min(o[0], 4 - o[0]) - min(o[1], 4 - o[1]),
    )
    band_peers = [
        (4 * i + j, lax.rem(grp // 4 + i, 4) * 4 + lax.rem(lax.rem(grp, 4) + j, 4)) for i, j in offsets
    ]

    barrier = pltpu.get_barrier_semaphore()
    for _, q in slab_peers:
        pl.semaphore_signal(barrier, inc=1, device_id={"slab": q}, device_id_type=MESH)
    for _, q in band_peers:
        pl.semaphore_signal(barrier, inc=1, device_id={"band": q}, device_id_type=MESH)

    def load(i):
        at = pl.ds(i * 2 * XROWS, 2 * XROWS)
        return pltpu.make_async_copy(orb.at[at], ib.at[at], in_sem.at[i])

    def table(i):
        return pltpu.make_async_copy(sources[i], consts[i], const_sem.at[i])

    table(0).start()
    table(1).start()
    for i in range(OWN // 2):
        load(i).start()
    for i in range(2, len(NAMES)):
        table(i).start()
    table(0).wait()
    table(1).wait()

    def slab_copy(src, dst, s, r, q):
        return pltpu.make_async_remote_copy(src, dst, s, r, device_id={"slab": q}, device_id_type=MESH)

    def band_copy(src, dst, s, r, q):
        return pltpu.make_async_remote_copy(src, dst, s, r, device_id={"band": q}, device_id_type=MESH)

    def row_of(pair):
        return pair // 2 * 8 + lax.rem(pair, 2) * 2

    def quad(ref, b, q, k):
        return ref.reshape(BANDS * SLABS * TILES, 24, 128).at[pl.ds((b * SLABS + q) * TILES, TILES), pl.ds(pl.multiple_of(8 * k, 8), 8)]

    def quad_copy(src, dst, b, k, d, q, send, recv):
        return slab_copy(quad(src, b, q, k), quad(dst, b, me, k), send.at[0], recv.at[k], q)

    def send_first(k, d, q):
        return quad_copy(wire, lines, 0, k, d, q, w_s, first_r)

    def send_last(k, d, q):
        return quad_copy(back, home, BANDS - 1, k, d, q, b_s, last_r)

    def done(view, sem):
        pltpu.make_async_copy(view, view, sem).wait()

    def rows(ref, n):
        return ref.at[pl.ds(0, n)]

    OTHERS, REST = SLABS - 1, GROUPS - 1

    def first(b, carry):
        def local(pair, carry):
            @pl.when(b == 0)
            def _():
                load(pair).wait()

            tiles = [
                jnp.concatenate(
                    [ib[pl.ds((2 * pair + i) * XROWS + 4 * t + b, PAIRS, stride=12), :] for i in range(2)], 0
                )
                for t in range(3)
            ]
            z = []
            for j in range(2):
                x = jnp.concatenate([tiles[j], tiles[j + 1]], 1)
                z.append(times2(x, z_in[pl.ds(256 * j, 256)]))
            x = jnp.concatenate(
                [
                    jnp.concatenate(
                        [z[j][48 * i : 48 * i + 48, 128 * c : 128 * c + 128] for j in range(2) for c in range(2)], 0
                    )
                    for i in range(2)
                ],
                1,
            )
            r = left2(y_in[...], x)
            for i in range(2):
                x = 2 * pair + i
                tiles = packed([r[48 * j : 48 * j + 48, 128 * i : 128 * i + 128] for j in range(4)])
                for t in range(3):
                    for c in range(2):
                        wire[pl.ds(b * BAND + t * 24 + 4 * c + row_of(pair) + i, 24, stride=72), :] = tiles[t][24 * c : 24 * c + 24]

            @pl.when((b == 0) & (pair == 1))
            def _():
                pl.semaphore_wait(barrier, SLABS - 1 + GROUPS - 1)

            @pl.when((b == 0) & (lax.rem(pair, 2) == 1))
            def _():
                for d, q in slab_peers:
                    send_first(pair // 2, d, q).start()

            return carry

        lax.fori_loop(0, OWN // 2, local, 0)

        @pl.when((b > 0) & (b < BANDS - 1))
        def _():
            for d, q in slab_peers:
                send_line(b, d, q).start()

        @pl.when(b == BANDS - 1)
        def _():
            for a in range(3):
                for d, q in slab_peers:
                    send_tail(a, d, q).start()

        own_line(b).start()
        return carry

    def send_tail(a, d, q):
        return slab_copy(
            wire.at[pl.ds((BANDS - 1) * BAND + q * BLOCK + 24 * CHUNKS[a][0], 24 * CHUNKS[a][1])],
            lines.at[pl.ds((BANDS - 1) * BAND + me * BLOCK + 24 * CHUNKS[a][0], 24 * CHUNKS[a][1])],
            w_s.at[0],
            tail_r.at[a],
            q,
        )

    def send_line(b, d, q):
        return slab_copy(
            wire.at[pl.ds(b * BAND + q * BLOCK, BLOCK)],
            lines.at[pl.ds(b * BAND + me * BLOCK, BLOCK)],
            w_s.at[0],
            w_r.at[b],
            q,
        )

    def own_line(b):
        at = pl.ds(b * BAND + me * BLOCK, BLOCK)
        return pltpu.make_async_copy(wire.at[at], lines.at[at], own_sem.at[b])

    lax.fori_loop(0, BANDS, first, 0)

    def send_pot(d, q):
        return slab_copy(
            pot.at[:, pl.ds(pl.multiple_of(q * LINE, 128), LINE)], vb.at[me], pot_s.at[0], pot_r.at[0], q
        )

    for d, q in slab_peers:
        send_pot(d, q).start()
    own_pot = pltpu.make_async_copy(
        pot.at[:, pl.ds(pl.multiple_of(me * LINE, 128), LINE)], vb.at[me], own_sem.at[BANDS]
    )
    own_pot.start()

    for i in range(2, len(NAMES)):
        table(i).wait()

    for i in range(8):
        ksq = ky2[...] + kxz[grp, i : i + 1, :]
        zero = ksq == 0.0
        green[:, 128 * i : 128 * i + 128] = jnp.where(zero, 0.0, 4.0 * math.pi / jnp.where(zero, 1.0, ksq))

    dens[...] = jnp.zeros_like(dens)

    def kx_in(b, start, count):
        x = jnp.concatenate(
            [
                jnp.concatenate(
                    [lines[pl.ds(b * BAND + s * BLOCK + (start + t) * 24, 24)] for s in range(SLABS)], 0
                )
                for t in range(count)
            ],
            1,
        )
        r = left2(x_in[...], x)
        at = pl.ds(pl.multiple_of(start * 128, 128), 128 * count)
        moved[b, :, at] = r
        dens[:, at] += r[:GRID] * r[:GRID] + r[GRID:] * r[GRID:]

    def lines_x(b, carry):
        own_line(b).wait()

        @pl.when(b == 0)
        def _():
            for k in range(3):
                done(rows(lines, OTHERS * 72), first_r.at[k])

        @pl.when(b > 0)
        def _():
            done(rows(lines, OTHERS * BLOCK), w_r.at[b])

        def chunk(a, carry):
            kx_in(b, 3 * a, 3)
            return carry

        lax.fori_loop(0, 3, chunk, 0)
        return carry

    lax.fori_loop(0, BANDS - 1, lines_x, 0)

    def lanes(a):
        return pl.ds(128 * CHUNKS[a][0], 128 * CHUNKS[a][1])

    def send_part(a, d, q):
        at = lanes(a)
        return band_copy(dq.at[pl.ds(pl.multiple_of(q * 8, 8), 8), at], part.at[grp, :, at], rs_s.at[0], rs_r.at[a], q)

    own_line(BANDS - 1).wait()

    for a in range(3):
        done(rows(lines, OTHERS * 24 * CHUNKS[a][1]), tail_r.at[a])
        kx_in(BANDS - 1, *CHUNKS[a])
        at = lanes(a)
        dq[:, at] = left(qx[pl.ds(0, 128)], qx[pl.ds(128, 128)], dens[:, at])
        for d, q in band_peers:
            send_part(a, d, q).start()

    own_pot.wait()
    done(rows(vb, OTHERS), pot_r.at[0])
    for s in range(SLABS):
        vl[OWN * s : OWN * s + OWN, :] = vb[s]

    def send_share(a, d, q):
        at = lanes(a)
        return slab_copy(share.at[:, at], whole.at[me, :, at], ag_s.at[0], ag_r.at[a], q)

    for a in range(3):
        at = lanes(a)
        done(part.at[pl.ds(0, REST), :, at], rs_r.at[a])
        total = dq[pl.ds(pl.multiple_of(grp * 8, 8), 8), at]
        for d, q in band_peers:
            total = total + part[q, :, at]
        share[:, at] = total
        for d, q in slab_peers:
            send_share(a, d, q).start()
        whole[me, :, at] = total

    for a in range(3):
        done(whole.at[pl.ds(0, OTHERS), :, lanes(a)], ag_r.at[a])
        tiles = [
            jnp.concatenate(
                [whole[s, :, 384 * a + 128 * t : 384 * a + 128 * t + 128] for s in range(SLABS)], 0
            )
            for t in range(3)
        ]
        x = jnp.concatenate(unpacked(tiles), 0)
        zt[pl.ds(256 * a, 256)] = times(x, qz[pl.ds(0, 128)], qz[pl.ds(128, 128)])
    x = jnp.concatenate([zt[pl.ds(i, GRID, stride=8), :] for i in range(8)], 1)
    x = left(qy[pl.ds(0, GRID)], qy[pl.ds(GRID, GRID)], x) * green[...]
    x = left(qyt[me, 0:16], qyt[me, 16:32], x)
    x = jnp.concatenate([x[:, 128 * i : 128 * i + 128] for i in range(8)], 0)
    zt[pl.ds(0, 128)] = times(x, qzt[pl.ds(0, 128)], qzt[pl.ds(128, 128)])
    for a in range(3):
        tiles = packed([zt[pl.ds(4 * a + j, 8, stride=16), :] for j in range(4)])
        for t in range(3):
            modes[SHARE * (3 * a + t) : SHARE * (3 * a + t) + 8, :] = tiles[t]

    def send_modes(k, d, q):
        start, rows = PIECES[k]
        return band_copy(
            modes.at[pl.ds(start, rows)],
            hq.at[pl.ds(grp * MODES + start, rows)],
            hq_s.at[0],
            hq_r.at[k],
            q,
        )

    for k in range(3):
        for d, q in band_peers:
            send_modes(k, d, q).start()
    hq[pl.ds(pl.multiple_of(grp * MODES, 8), MODES)] = modes[...]

    def send_back(b, d, q):
        return slab_copy(
            back.at[pl.ds(b * BAND + q * BLOCK, BLOCK)],
            home.at[pl.ds(b * BAND + me * BLOCK, BLOCK)],
            b_s.at[0],
            b_r.at[b],
            q,
        )

    def own_back(b):
        at = pl.ds(b * BAND + me * BLOCK, BLOCK)
        return pltpu.make_async_copy(back.at[at], home.at[at], own_sem.at[b])

    def send_head(a, d, q):
        return slab_copy(
            back.at[pl.ds(q * BLOCK + 24 * HEADS[a][0], 24 * HEADS[a][1])],
            home.at[pl.ds(me * BLOCK + 24 * HEADS[a][0], 24 * HEADS[a][1])],
            b_s.at[0],
            head_r.at[a],
            q,
        )

    def kx_out(b, start, count):
        at = pl.ds(pl.multiple_of(start * 128, 128), 128 * count)
        re = moved[b, 0:GRID, at]
        im = moved[b, GRID : 2 * GRID, at]
        cs = cosb[:, at]
        sn = sinb[:, at]
        x = jnp.concatenate([re * cs + im * sn, im * cs - re * sn], 0)
        r = left2(x_out[...], x)
        for q in range(SLABS):
            for t in range(count):
                back[pl.ds(b * BAND + q * BLOCK + (start + t) * 24, 24)] = r[24 * q : 24 * q + 24, 128 * t : 128 * t + 128]

    for a in range(3):
        done(rows(hq, REST * PIECES[a][1]), hq_r.at[a])
        at = pl.ds(128 * HEADS[a][0], 128 * HEADS[a][1])
        x = jnp.concatenate(
            [
                jnp.concatenate(
                    [
                        hq[MODES * g + SHARE * t : MODES * g + SHARE * t + 8, :]
                        for g in range(GROUPS)
                    ],
                    0,
                )
                for t in range(HEADS[a][0], sum(HEADS[a]))
            ],
            1,
        )
        h = left(qxt[pl.ds(0, GRID)], qxt[pl.ds(GRID, GRID)], x)
        hart[:, at] = h
        s, c = sin_cos((vl[:, at] + h) * TIME_STEP + OFFSET)
        sinb[:, at] = s * SCALE**6
        cosb[:, at] = c * SCALE**6
        kx_out(0, *HEADS[a])
        for d, q in slab_peers:
            send_head(a, d, q).start()
    own_back(0).start()

    for t in range(TILES):
        hs[pl.ds(t, GRID, stride=16), :] = hart[:, 128 * t : 128 * t + 128]

    def send_row(d, q):
        return slab_copy(
            hs.at[pl.ds((q * OWN + grp) * 16, 16)],
            hrow.at[pl.ds((grp * SLABS + me) * 16, 16)],
            h_s.at[0],
            h_r.at[0],
            q,
        )

    own_row = pltpu.make_async_copy(
        hs.at[pl.ds((me * OWN + grp) * 16, 16)], hrow.at[pl.ds((grp * SLABS + me) * 16, 16)], own_sem.at[BANDS]
    )

    def send_rows(d, q, g):
        at = pl.ds(g * (SLABS * 16), SLABS * 16)
        return band_copy(hrow.at[at], hrow.at[at], g_s.at[0], g_r.at[0], q)

    @pl.when(grp < OWN)
    def _():
        own_row.start()
        for d, q in slab_peers:
            send_row(d, q).start()

    def kick(b, carry):
        def chunk(a, carry):
            kx_out(b, 3 * a, 3)
            return carry

        lax.fori_loop(0, 3, chunk, 0)
        @pl.when(b < BANDS - 1)
        def _():
            for d, q in slab_peers:
                send_back(b, d, q).start()

        @pl.when(b == BANDS - 1)
        def _():
            for k in range(3):
                for d, q in slab_peers:
                    send_last(k, d, q).start()

        own_back(b).start()
        return carry

    lax.fori_loop(1, BANDS, kick, 0)

    def rows_out():
        @pl.when(grp < OWN)
        def _():
            own_row.wait()
            done(rows(hrow, OTHERS * 16), h_r.at[0])
            for d, q in band_peers:
                send_rows(d, q, grp).start()

    def rows_in():
        @pl.when(grp < OWN)
        def _():
            done(rows(hrow, (OWN - 1) * SLABS * 16), g_r.at[0])

        @pl.when(grp >= OWN)
        def _():
            done(rows(hrow, OWN * SLABS * 16), g_r.at[0])

        for s in range(SLABS):
            for t in range(TILES):
                har[:, LINE * s + 128 * t : LINE * s + 128 * t + 128] = hrow[
                    pl.ds(16 * s + t, OWN, stride=SLABS * 16), :
                ]

    def last(b, carry):
        @pl.when(b == 1)
        def _():
            rows_out()

        @pl.when(b == 3)
        def _():
            rows_in()

        own_back(b).wait()

        @pl.when(b == 0)
        def _():
            for a in range(3):
                done(rows(home, OTHERS * 24 * HEADS[a][1]), head_r.at[a])

        @pl.when((b > 0) & (b < BANDS - 1))
        def _():
            done(rows(home, OTHERS * BLOCK), b_r.at[b])

        def local(pair, carry):
            @pl.when((b == BANDS - 1) & (lax.rem(pair, 2) == 0))
            def _():
                done(rows(home, OTHERS * 72), last_r.at[pair // 2])

            cols = []
            for i in range(2):
                x = 2 * pair + i
                tiles = [
                    jnp.concatenate(
                        [home[pl.ds(b * BAND + t * 24 + 4 * c + row_of(pair) + i, 24, stride=72), :] for c in range(2)], 0
                    )
                    for t in range(3)
                ]
                cols.append(jnp.concatenate(unpacked(tiles), 0))
            r = left2(y_out[...], jnp.concatenate(cols, 1))
            res = []
            for j in range(2):
                x = jnp.concatenate(
                    [
                        jnp.concatenate(
                            [r[96 * j + 48 * c : 96 * j + 48 * c + 48, 128 * i : 128 * i + 128] for c in range(2)], 1
                        )
                        for i in range(2)
                    ],
                    0,
                )
                res.append(times2(x, z_out[pl.ds(256 * j, 256)]))
            tiles = (res[0][:, :128], res[0][:, 128:] + res[1][:, :128], res[1][:, 128:])
            for i in range(2):
                for t in range(3):
                    ev[pl.ds((2 * pair + i) * XROWS + 4 * t + b, PAIRS, stride=12), :] = tiles[t][48 * i : 48 * i + 48]

            return carry

        lax.fori_loop(0, OWN // 2, local, 0)
        return carry

    lax.fori_loop(0, BANDS, last, 0)

    @pl.when(grp < OWN)
    def _():
        done(rows(hs, OTHERS * 16), h_s.at[0])
        done(rows(wire, REST * SLABS * 16), g_s.at[0])

    done(rows(vb, OTHERS), pot_s.at[0])
    done(rows(wire, 3 * OTHERS * 24), ag_s.at[0])
    done(rows(wire, 3 * REST * 24), rs_s.at[0])
    done(rows(wire, REST * MODES), hq_s.at[0])
    done(rows(wire, BANDS * OTHERS * BLOCK), w_s.at[0])
    done(rows(back, BANDS * OTHERS * BLOCK), b_s.at[0])


def result(ev, har, ev_out, har_out, sem):
    n = ev.shape[0] // 8
    copies = [
        pltpu.make_async_copy(ev.at[pl.ds(n * i, n)], ev_out.at[pl.ds(n * i, n)], sem.at[i]) for i in range(8)
    ]
    copies.append(pltpu.make_async_copy(har, har_out, sem.at[8]))
    for copy in copies:
        copy.start()
    for copy in copies:
        copy.wait()


def body(orbitals, potential):
    rows = orbitals.reshape(BANDS, OWN, XROWS // BANDS, 128).transpose(1, 2, 0, 3).reshape(OWN * XROWS, 128)
    t = tables()
    consts = [jnp.asarray(t[name]) for name in NAMES]
    vmem = lambda *shape: pltpu.VMEM(shape, F32)
    dma = lambda *shape: pltpu.SemaphoreType.DMA(shape)
    ev, har = pl.pallas_call(
        kernel,
        out_shape=(
            pltpu.VMEM((OWN * XROWS, 128), F32),
            pltpu.VMEM(potential.shape, F32),
        ),
        in_specs=[pl.BlockSpec(memory_space=pl.ANY)] * (2 + len(consts)),
        out_specs=[pl.BlockSpec(memory_space=pltpu.VMEM)] * 2,
        scratch_shapes=[pltpu.VMEM(c.shape, c.dtype) for c in consts]
        + [
            vmem(OWN * XROWS, 128),
            vmem(BANDS * BAND, 128),
            vmem(BANDS * BAND, 128),
            vmem(BANDS, 2 * GRID, LINE),
            vmem(BANDS * BAND, 128),
            vmem(BANDS * BAND, 128),
            vmem(GRID, LINE),
            vmem(128, LINE),
            vmem(GROUPS, 8, LINE),
            vmem(8, LINE),
            vmem(MODES, 128),
            vmem(SLABS, 8, LINE),
            vmem(768, 128),
            vmem(GRID, 1024),
            vmem(GROUPS * MODES, 128),
            vmem(GRID, LINE),
            vmem(SLABS, OWN, LINE),
            vmem(GRID, LINE),
            vmem(GRID, LINE),
            vmem(GRID, LINE),
            vmem(GRID * 16, 128),
            vmem(OWN * SLABS * 16, 128),
            dma(OWN // 2),
            dma(1), dma(1),
            dma(1), dma(BANDS),
            dma(1), dma(BANDS),
            dma(1), dma(3),
            dma(1), dma(3),
            dma(1), dma(3),
            dma(1), dma(1),
            dma(1), dma(1),
            dma(BANDS + 1),
            dma(len(consts)),
            dma(3), dma(3), dma(3), dma(3),
        ],
        compiler_params=pltpu.CompilerParams(
            collective_id=0, has_side_effects=True, vmem_limit_bytes=60416 * 1024
        ),
    )(rows, potential, *consts)
    ev, har = pl.pallas_call(
        result,
        out_shape=(jax.ShapeDtypeStruct(ev.shape, F32), jax.ShapeDtypeStruct(har.shape, F32)),
        in_specs=[pl.BlockSpec(memory_space=pltpu.VMEM)] * 2,
        out_specs=[pl.BlockSpec(memory_space=pl.ANY)] * 2,
        scratch_shapes=[pltpu.SemaphoreType.DMA((9,))],
        compiler_params=pltpu.CompilerParams(vmem_limit_bytes=1024 * 1024),
    )(ev, har)
    return ev.reshape(OWN, XROWS // BANDS, BANDS, 128).transpose(2, 0, 1, 3).reshape(orbitals.shape), har


def solution(mesh):
    return jax.shard_map(
        body,
        mesh=mesh,
        in_specs=(P("band", "slab", None), P("slab", None)),
        out_specs=(P("band", "slab", None), P("slab", None)),
        check_vma=False,
    )
```
